512 devices in a mesh: tile: 128 (over z, y, core), chan: 4 (over x).
Axes of the slice: x: 4, y: 8, z: 8, core: 2. Of those that a mesh axis runs over, the one named last changes fastest.
Arguments:
- features: bfloat16 [128, 192, 2304], P('tile', 'chan'), may hold values from -6 to 6
- land_mask: int32 [128, 2304], P('tile'), may hold values 0 or 1
- wet_slots: int32 [128], replicated, may hold values from 0 to 255, as said below
- device_of: int32 [128], replicated, may hold values from 0 to 127, as said below
- depth_weight: float32 [2, 192, 49], P(None, 'chan'), may hold values from -0.875 to 0.875
- depth_bias: float32 [2, 192], P(None, 'chan'), may hold values from -1.5 to 1.5
- norm_gain: float32 [2, 192], replicated, may hold values from 0.5 to 1.5
- norm_bias: float32 [2, 192], replicated, may hold values from -1.5 to 1.5
- up_weight: bfloat16 [2, 768, 192], replicated, may hold values from -0.4375 to 0.4375
- up_bias: float32 [2, 768], replicated, may hold values from -2.5 to 2.5
- down_weight: bfloat16 [2, 192, 768], replicated, may hold values from -0.21875 to 0.21875
- down_bias: float32 [2, 192], replicated, may hold values from -1.5 to 1.5
- layer_scale: float32 [2, 192], P(None, 'chan'), may hold values from 0.5 to 1.5
- pool_weight: float32 [192, 4], P('chan'), may hold values from -2.5 to 2.5
- spread_weight: float32 [192, 4], P('chan'), may hold values from -2.5 to 2.5
Outputs:
- merged: bfloat16 [128, 192, 2304], P('tile', 'chan')
The draws below stay inside these ranges and needn't reach their ends.
Inputs may be any that keep to these rules, and one draw needn't show every extreme that they name: `wet_slots`: 128 distinct grid slots in increasing order, among them slots 0, 1 and the last slot. `device_of`: each device along tile holds exactly one wet tile; the tiles in slots 0 and 1 lie 128 / 2 devices apart, counted round. `land_mask`: 1 marks an ocean cell, 0 a land cell.
All inputs are finite; a program needn't handle non-finite values. No bound on the sum of `land_mask` on one device may be relied on, other than what follows from the above.
Results may differ from the reference program's by a relative error of at most 0.011.
Values may be sent and summed in bfloat16 or wider, within the bound.
A program may use at most 64 MiB of HBM per device.

```python
import jax
import jax.numpy as jnp
from jax import lax

CHANNELS = 192
HIDDEN_SIZE = 768
TILE = 48
GRID_Y = 4
LEVELS = 2
GRID_X = 64
WET = 128


def draw_wet_slots(key, part):
    slot_count = GRID_X * GRID_Y
    scores = jax.random.permutation(key, slot_count).astype(jnp.int32)
    slot_ids = jnp.arange(slot_count, dtype=jnp.int32)
    scores = jnp.where(slot_ids == 0, slot_count, scores)
    scores = jnp.where(slot_ids == 1, slot_count + 2, scores)
    scores = jnp.where(slot_ids == slot_count - 1, slot_count + 1, scores)
    best_scores, chosen = lax.top_k(scores, WET)
    return jnp.sort(chosen).astype(jnp.int32)


def draw_device_of(key, part):
    order = jax.random.permutation(key, WET).astype(jnp.int32)
    positions = jnp.arange(WET, dtype=jnp.int32)
    target = (order[0] + WET // 2) % WET
    where_target = jnp.sum(jnp.where(order == target, positions, 0)).astype(jnp.int32)
    second = order[1]
    swapped = jnp.where(positions == 1, target, order)
    swapped = jnp.where(positions == where_target, second, swapped)
    swapped = jnp.where(positions == 1, target, swapped)
    return swapped.astype(jnp.int32)


def plant(values, key, least, top_value):
    longest = values.shape.index(max(values.shape))
    spots = []
    for shift in (0, 1):
        where = [jax.random.randint(jax.random.fold_in(key, axis), (), 0, length) for axis, length in enumerate(values.shape)]
        where[longest] = (where[longest] + shift) % values.shape[longest]
        spots.append(tuple(where))
    return values.at[spots[0]].set(least).at[spots[1]].set(top_value)


def levels(stream_key, extent, split, least, high):
    def one(dim, parts):
        steps = jax.random.uniform(jax.random.fold_in(jax.random.fold_in(stream_key, 6), dim), (parts,), jnp.float32, least / len(split), high / len(split))
        return jnp.repeat(jnp.exp(steps), extent[dim] // parts).reshape((-1,) + (1,) * (len(extent) - dim - 1))

    factor_of = one(*split[0])
    for cut in split[1:]:
        factor_of = factor_of * one(*cut)
    return factor_of


def noise(stream_key, shape, scale, bound, shards=(), kind=jnp.bfloat16):
    gain = levels(stream_key, shape, shards, -0.22, 0.18) if shards else 1.0
    values = jax.random.normal(stream_key, shape, jnp.float32) * scale * gain
    return jnp.minimum(jnp.maximum(values, -bound), bound).astype(kind)


def setup_inputs(seed: int = 0) -> dict:
    key_list = jax.random.split(jax.random.key(seed), 16)
    return {
        "features": noise(key_list[0], (WET, CHANNELS, TILE * TILE), 1.0, 6.0, ((0, 128), (1, 4))),
        "land_mask": plant((jax.random.randint(key_list[1], (WET, TILE * TILE), 0, 8) < 7).astype(jnp.int32), jax.random.fold_in(key_list[1], 1), 0, 1),
        "wet_slots": draw_wet_slots(jax.random.fold_in(key_list[15], 71), 0),
        "device_of": draw_device_of(jax.random.fold_in(key_list[15], 71), 0),
        "depth_weight": noise(key_list[4], (LEVELS, CHANNELS, 49), 49 ** -0.5, 0.875, ((1, 4),), jnp.float32),
        "depth_bias": noise(key_list[5], (LEVELS, CHANNELS), 0.3, 1.5, ((1, 4),), jnp.float32),
        "norm_gain": jnp.clip(1.0 + 0.1 * jax.random.normal(key_list[6], (LEVELS, CHANNELS), jnp.float32), 0.5, 1.5),
        "norm_bias": noise(key_list[7], (LEVELS, CHANNELS), 0.3, 1.5, (), jnp.float32),
        "up_weight": noise(key_list[8], (LEVELS, HIDDEN_SIZE, CHANNELS), CHANNELS ** -0.5, 0.4375),
        "up_bias": noise(key_list[9], (LEVELS, HIDDEN_SIZE), 0.5, 2.5, (), jnp.float32),
        "down_weight": noise(key_list[10], (LEVELS, CHANNELS, HIDDEN_SIZE), HIDDEN_SIZE ** -0.5, 0.21875),
        "down_bias": noise(key_list[11], (LEVELS, CHANNELS), 0.3, 1.5, (), jnp.float32),
        "layer_scale": jnp.clip(1.0 + 0.1 * jax.random.normal(key_list[12], (LEVELS, CHANNELS), jnp.float32), 0.5, 1.5),
        "pool_weight": noise(key_list[13], (CHANNELS, 4), 0.5, 2.5, ((0, 4),), jnp.float32),
        "spread_weight": noise(key_list[14], (CHANNELS, 4), 0.5, 2.5, ((0, 4),), jnp.float32),
    }


BANDS = ((-1, -1), (-1, 0), (-1, 1), (0, -1), (0, 1), (1, -1), (1, 0), (1, 1))
norm_eps = 1e-06

def neighbour_tables(wet_slots, device_of, grid_x, grid_y):
    tile_count = wet_slots.shape[0]
    devices = jnp.arange(tile_count, dtype=jnp.int32)
    holder = device_of[:, None] == devices[None, :]
    device_slot = lax.optimization_barrier(jnp.sum(jnp.where(holder, wet_slots[:, None], 0), axis=0)).astype(jnp.int32)
    slot_ids = jnp.arange(grid_x * grid_y, dtype=jnp.int32)
    owned = device_slot[:, None] == slot_ids[None, :]
    slot_device = (lax.optimization_barrier(jnp.sum(jnp.where(owned, devices[:, None] + 1, 0), axis=0)) - 1).astype(jnp.int32)
    column = device_slot % grid_x
    tile_row = device_slot // grid_x
    sources = []
    strip_ids = []
    flips = []
    for up_by, right_by in BANDS:
        near_column = (column + right_by) % grid_x
        near_row = tile_row + up_by
        folded = near_row >= grid_y
        source_column = jnp.where(folded, grid_x - 1 - near_column, near_column)
        source_row = jnp.where(folded, grid_y - 1, near_row)
        source_slot = source_row * grid_x + source_column
        matched = source_slot[:, None] == slot_ids[None, :]
        source = (lax.optimization_barrier(jnp.sum(jnp.where(matched, slot_device[None, :] + 1, 0), axis=1)) - 1).astype(jnp.int32)
        source = jnp.where(near_row < 0, -1, source).astype(jnp.int32)
        if up_by == -1:
            strip_id = jnp.full_like(column, 1)
        elif up_by == 1:
            strip_id = jnp.where(folded, 1, 0).astype(jnp.int32)
        elif right_by == -1:
            strip_id = jnp.full_like(column, 3)
        else:
            strip_id = jnp.full_like(column, 2)
        sources.append(source)
        strip_ids.append(strip_id.astype(jnp.int32))
        flips.append(folded)
    return (jnp.stack(sources, axis=1), jnp.stack(strip_ids, axis=1), jnp.stack(flips, axis=1))

def edge_strips(tile_grid):
    tile_side = tile_grid.shape[-1]
    first_rows = tile_grid[..., :3, :]
    last_rows = tile_grid[..., tile_side - 3:, :]
    first_cols = jnp.swapaxes(tile_grid[..., :, :3], -1, -2)
    last_cols = jnp.swapaxes(tile_grid[..., :, tile_side - 3:], -1, -2)
    return jnp.stack([first_rows, last_rows, first_cols, last_cols], axis=-4)

def padded_tile(own_tile, raw_strips, flips):
    tile_side = own_tile.shape[-1]
    band_list = []
    for band_index, (up_by, right_by) in enumerate(BANDS):
        piece_in = raw_strips[band_index]
        if up_by != 0:
            if up_by == 1:
                piece_in = jnp.where(flips[band_index], piece_in[:, ::-1, ::-1], piece_in)
            if right_by == -1:
                piece_in = piece_in[:, :, tile_side - 3:]
            elif right_by == 1:
                piece_in = piece_in[:, :, :3]
        else:
            piece_in = jnp.swapaxes(piece_in, 1, 2)
        band_list.append(piece_in)
    lower_rows = jnp.concatenate([band_list[0], band_list[1], band_list[2]], axis=2)
    middle_rows = jnp.concatenate([band_list[3], own_tile, band_list[4]], axis=2)
    upper_rows = jnp.concatenate([band_list[5], band_list[6], band_list[7]], axis=2)
    return jnp.concatenate([lower_rows, middle_rows, upper_rows], axis=1)

def depthwise(padded, weights, bias_row):
    chan_rows = padded.shape[0]
    padded_side = padded.shape[1]
    tile_side = padded_side - 6
    flat_cells = padded.astype(jnp.float32).reshape(chan_rows, padded_side * padded_side)
    flat_cells = jnp.pad(flat_cells, ((0, 0), (0, 6)))
    span_cells = tile_side * padded_side
    running = jnp.zeros((chan_rows, span_cells), jnp.float32)
    for row_step in range(7):
        for col_step in range(7):
            offset = row_step * padded_side + col_step
            running = running + weights[:, row_step * 7 + col_step][:, None] * flat_cells[:, offset:offset + span_cells]
    conv_out = running.reshape(chan_rows, tile_side, padded_side)[:, :, :tile_side] + bias_row[:, None, None]
    return conv_out.astype(jnp.bfloat16)

def mixed_branch(block_in, params, row_start, row_count):
    values = block_in.astype(jnp.float32)
    cell_mean = lax.optimization_barrier(jnp.mean(values, axis=0, keepdims=True))
    centred = values - cell_mean
    spread = lax.optimization_barrier(jnp.mean(centred * centred, axis=0, keepdims=True))
    normed = (centred * lax.rsqrt(spread + norm_eps) * params[2][:, None] + params[3][:, None]).astype(jnp.bfloat16)
    hidden = jnp.dot(params[4], normed, preferred_element_type=jnp.float32) + params[5][:, None]
    hidden = jax.nn.gelu(hidden, approximate=False).astype(jnp.bfloat16)
    down_rows = lax.dynamic_slice_in_dim(params[6], row_start, row_count, 0)
    bias_rows = lax.dynamic_slice_in_dim(params[7], row_start, row_count, 0)
    return jnp.dot(down_rows, hidden, preferred_element_type=jnp.float32) + bias_rows[:, None]

def pool_cells(tile_grid, weights):
    values = tile_grid.astype(jnp.float32)
    running = weights[:, 0][:, None, None] * values[:, 0::2, 0::2]
    running = running + weights[:, 1][:, None, None] * values[:, 0::2, 1::2]
    running = running + weights[:, 2][:, None, None] * values[:, 1::2, 0::2]
    running = running + weights[:, 3][:, None, None] * values[:, 1::2, 1::2]
    return running.astype(jnp.bfloat16)

def coarse_mask(mask_grid):
    half_side = mask_grid.shape[0] // 2
    return lax.optimization_barrier(jnp.max(mask_grid.reshape(half_side, 2, half_side, 2), axis=(1, 3)))

def join_levels(fine_flat, coarse_flat, weights, cell_mask, tile_side):
    chan_rows = fine_flat.shape[0]
    half_side = tile_side // 2
    coarse_vals = coarse_flat.astype(jnp.float32).reshape(chan_rows, half_side, half_side)
    spread = weights.reshape(chan_rows, 2, 2)
    expanded = coarse_vals[:, :, None, :, None] * spread[:, None, :, None, :]
    expanded = expanded.reshape(chan_rows, tile_side * tile_side)
    return (cell_mask[None, :] * (fine_flat.astype(jnp.float32) + expanded)).astype(jnp.bfloat16)

def level_reference(tiles, tile_side, params, masks, tables):
    tile_count = tiles.shape[0]
    channels_all = tiles.shape[1]
    tile_grid = tiles.reshape(tile_count, channels_all, tile_side, tile_side)
    strip_table = edge_strips(tile_grid)
    sources, strip_ids, flips = tables

    def one_tile(device):
        my_sources = sources[device]
        my_strips = strip_ids[device]
        raw_strips = []
        for band_index in range(8):
            source = my_sources[band_index]
            picked = strip_table[jnp.maximum(source, 0), my_strips[band_index]]
            raw_strips.append(jnp.where(source >= 0, picked, jnp.zeros_like(picked)))
        padded = padded_tile(tile_grid[device], raw_strips, flips[device])
        conv_out = depthwise(padded, params[0], params[1]).reshape(channels_all, tile_side * tile_side)
        branch = mixed_branch(conv_out, params, 0, channels_all)
        return (masks[device][None, :] * (tiles[device].astype(jnp.float32) + params[8][:, None] * branch)).astype(jnp.bfloat16)
    return lax.map(one_tile, jnp.arange(tile_count, dtype=jnp.int32))

def reference(features, land_mask, wet_slots, device_of, depth_weight, depth_bias, norm_gain, norm_bias, up_weight, up_bias, down_weight, down_bias, layer_scale, pool_weight, spread_weight):
    tables = neighbour_tables(wet_slots, device_of, GRID_X, GRID_Y)
    stacks = (depth_weight, depth_bias, norm_gain, norm_bias, up_weight, up_bias, down_weight, down_bias, layer_scale)
    fine_params = tuple((array[0] for array in stacks))
    coarse_params = tuple((array[1] for array in stacks))
    channels_all = features.shape[1]
    half_side = TILE // 2
    fine_masks = land_mask.astype(jnp.float32)
    fine_out = level_reference(features, TILE, fine_params, fine_masks, tables)

    def pool_one(tile_flat):
        return pool_cells(tile_flat.reshape(channels_all, TILE, TILE), pool_weight).reshape(channels_all, half_side * half_side)

    def mask_one(mask_flat):
        return coarse_mask(mask_flat.reshape(TILE, TILE)).reshape(half_side * half_side)
    pooled = jax.vmap(pool_one)(fine_out)
    coarse_masks = jax.vmap(mask_one)(land_mask).astype(jnp.float32)
    coarse = level_reference(pooled, half_side, coarse_params, coarse_masks, tables)

    def join_one(fine_flat, coarse_flat, mask_flat):
        return join_levels(fine_flat, coarse_flat, spread_weight, mask_flat, TILE)
    return jax.vmap(join_one)(fine_out, coarse, fine_masks)
```

```python
import functools

import jax
import jax.numpy as jnp
from jax import lax
from jax.experimental import pallas as pl
from jax.experimental.pallas import tpu as pltpu
from jax.sharding import PartitionSpec as P

TILE = 48
GRID_Y = 4
MESH = pl.DeviceIdType.MESH
BANDS = ((-1, -1), (-1, 0), (-1, 1), (0, -1), (0, 1), (1, -1), (1, 0), (1, 1))
norm_eps = 1e-06
VMEM_SPEC = pl.BlockSpec(memory_space=pltpu.VMEM)


def pick_table(wet_slots, device_of, grid_x, grid_y):
    tile_count = wet_slots.shape[0]
    devices = jnp.arange(tile_count, dtype=jnp.int32)
    slot = jnp.sum(jnp.where(device_of[None, :] == devices[:, None], wet_slots[None, :], 0), axis=1)
    column = slot % grid_x
    tile_row = slot // grid_x
    up = jnp.array([b[0] for b in BANDS], jnp.int32)[None, :]
    right = jnp.array([b[1] for b in BANDS], jnp.int32)[None, :]
    near_column = (column[:, None] + right) % grid_x
    near_row = tile_row[:, None] + up
    folded = near_row >= grid_y
    source_column = jnp.where(folded, grid_x - 1 - near_column, near_column)
    source_row = jnp.where(folded, grid_y - 1, near_row)
    source_slot = jnp.where(near_row < 0, -1, source_row * grid_x + source_column)
    strip = jnp.where(up == -1, 1, jnp.where(up == 1, jnp.where(folded, 1, 0), jnp.where(right == -1, 3, 2)))
    row_of_tile = device_of * 4 + 1
    found = jnp.sum(
        jnp.where(source_slot[:, :, None] == wet_slots[None, None, :], row_of_tile[None, None, :], 0), axis=2
    )
    table = jnp.where(found > 0, found - 1 + strip, tile_count * 4).astype(jnp.int32)
    return table, tile_row >= grid_y - 1


def halo_kernel(tiles, pieces, table_ref, strips_ref, got_ref, held, picked, send_a, recv_a, send_b, recv_b):
    me = lax.axis_index("tile")
    piece = (me * pieces + tiles - 1) // tiles
    holds = jnp.logical_and(piece < pieces, (piece * tiles) // pieces == me)
    holder = lambda p: (p * tiles) // pieces
    barrier = pltpu.get_barrier_semaphore()

    @pl.when(holds)
    def _():
        @pl.loop(1, tiles)
        def _(k):
            pl.semaphore_signal(barrier, inc=1, device_id={"tile": lax.rem(me + k, tiles)}, device_id_type=MESH)

        pl.semaphore_wait(barrier, tiles - 1)

    @pl.when(jnp.logical_not(holds))
    def _():
        @pl.loop(0, pieces)
        def _(p):
            pl.semaphore_signal(barrier, inc=1, device_id={"tile": holder(p)}, device_id_type=MESH)

        pl.semaphore_wait(barrier, pieces)

    @pl.loop(0, pieces)
    def _(p):
        target = holder(p)

        @pl.when(target != me)
        def _():
            pltpu.make_async_remote_copy(
                src_ref=strips_ref.at[p],
                dst_ref=held.at[pl.ds(me * 4, 4)],
                send_sem=send_a,
                recv_sem=recv_a,
                device_id={"tile": target},
                device_id_type=MESH,
            ).start()

    @pl.when(holds)
    def _():
        held[tiles * 4] = jnp.zeros(held.shape[1:], held.dtype)
        held[pl.ds(me * 4, 4)] = strips_ref[piece]
        everything = held.at[pl.ds(0, (tiles - 1) * 4)]
        pltpu.make_async_copy(everything, everything, recv_a).wait()

        @pl.loop(0, tiles)
        def _(k):
            target = lax.rem(me + k, tiles)
            for band in range(8):
                picked[target, band] = held[table_ref[target * 8 + band]]

            @pl.when(k > 0)
            def _():
                pltpu.make_async_remote_copy(
                    src_ref=picked.at[target],
                    dst_ref=got_ref.at[piece],
                    send_sem=send_b,
                    recv_sem=recv_b,
                    device_id={"tile": target},
                    device_id_type=MESH,
                ).start()

        got_ref[piece] = picked[me]
        others = strips_ref.at[pl.ds(0, pieces - 1)]
        pltpu.make_async_copy(others, others, send_a).wait()
        arrived = got_ref.at[pl.ds(0, pieces - 1)]
        pltpu.make_async_copy(arrived, arrived, recv_b).wait()
        left = picked.at[pl.ds(0, tiles - 1)]
        pltpu.make_async_copy(left, left, send_b).wait()

    @pl.when(jnp.logical_not(holds))
    def _():
        pltpu.make_async_copy(strips_ref, strips_ref, send_a).wait()
        pltpu.make_async_copy(got_ref, got_ref, recv_b).wait()


def exchange(strips, table, call_id):
    tiles = table.shape[0]
    length = strips.shape[1]
    pieces = -(-length // 256)
    padded = jnp.pad(strips, ((0, 0), (0, pieces * 256 - length)))
    cut = padded.reshape(4, pieces, 2, 128).transpose(1, 0, 2, 3)
    got = pl.pallas_call(
        functools.partial(halo_kernel, tiles, pieces),
        out_shape=jax.ShapeDtypeStruct((pieces, 8, 2, 128), jnp.bfloat16),
        in_specs=[pl.BlockSpec(memory_space=pltpu.SMEM), VMEM_SPEC],
        out_specs=VMEM_SPEC,
        scratch_shapes=[
            pltpu.VMEM((tiles * 4 + 1, 2, 128), jnp.bfloat16),
            pltpu.VMEM((tiles, 8, 2, 128), jnp.bfloat16),
            pltpu.SemaphoreType.DMA,
            pltpu.SemaphoreType.DMA,
            pltpu.SemaphoreType.DMA,
            pltpu.SemaphoreType.DMA,
        ],
        compiler_params=pltpu.CompilerParams(collective_id=call_id, has_side_effects=True),
        name=f"halo_{call_id}",
    )(table.reshape(-1), cut)
    return got.transpose(1, 0, 2, 3).reshape(8, pieces * 256)[:, :length]


def mix_kernel(
    ways, conv_ref, gain_ref, bias_ref, up_ref, upb_ref, down_ref, downb_ref, out_ref, every, acc, branch, sa, ra, sb, rb
):
    me = lax.axis_index("chan")
    barrier = pltpu.get_barrier_semaphore()
    for k in range(1, ways):
        pl.semaphore_signal(barrier, inc=1, device_id={"chan": lax.rem(me + k, ways)}, device_id_type=MESH)
    pl.semaphore_wait(barrier, ways - 1)
    copies = []
    for k in range(1, ways):
        peer = lax.rem(me + k, ways)
        copy = pltpu.make_async_remote_copy(
            src_ref=conv_ref.at[peer],
            dst_ref=every.at[me],
            send_sem=sa.at[k],
            recv_sem=ra.at[k],
            device_id={"chan": peer},
            device_id_type=MESH,
        )
        copy.start()
        copies.append(copy)
    every[me] = conv_ref[me]
    for copy in copies:
        copy.wait()
    values = every[...].astype(jnp.float32)
    group, rows, cells = values.shape
    count = group * rows
    mean = jnp.sum(jnp.sum(values, axis=0), axis=0, keepdims=True) * (1.0 / count)
    centred = values - mean[None]
    spread = jnp.sum(jnp.sum(centred * centred, axis=0), axis=0, keepdims=True) * (1.0 / count)
    scaled = (centred * lax.rsqrt(spread + norm_eps)[None]).reshape(count, cells)
    normed = (scaled * gain_ref[...] + bias_ref[...]).astype(jnp.bfloat16)
    acc[...] = jnp.broadcast_to(downb_ref[...], acc.shape)
    hidden_size = up_ref.shape[0]
    step = 256

    @pl.loop(0, hidden_size // step)
    def _(i):
        at = pl.multiple_of(i * step, step)
        hidden = jnp.dot(up_ref[pl.ds(at, step), :], normed, preferred_element_type=jnp.float32)
        hidden = hidden + upb_ref[pl.ds(at, step), :]
        hidden = 0.5 * hidden * (1.0 + lax.erf(hidden * (0.5**0.5)))
        acc[...] += jnp.dot(
            down_ref[:, pl.ds(at, step)], hidden.astype(jnp.bfloat16), preferred_element_type=jnp.float32
        )

    branch[...] = acc[...].astype(jnp.bfloat16).reshape(branch.shape)
    copies = []
    for k in range(1, ways):
        peer = lax.rem(me + k, ways)
        copy = pltpu.make_async_remote_copy(
            src_ref=branch.at[peer],
            dst_ref=out_ref.at[me],
            send_sem=sb.at[k],
            recv_sem=rb.at[k],
            device_id={"chan": peer},
            device_id_type=MESH,
        )
        copy.start()
        copies.append(copy)
    out_ref[me] = branch[me]
    for copy in copies:
        copy.wait()


def mix(conv, params, ways, call_id):
    rows, cells = conv.shape
    part = cells // ways
    cut = conv.reshape(rows, ways, part).transpose(1, 0, 2)
    shape = (ways, rows, part)
    out = pl.pallas_call(
        functools.partial(mix_kernel, ways),
        out_shape=jax.ShapeDtypeStruct(shape, jnp.bfloat16),
        in_specs=[VMEM_SPEC] * 7,
        out_specs=VMEM_SPEC,
        scratch_shapes=[
            pltpu.VMEM(shape, jnp.bfloat16),
            pltpu.VMEM((ways * rows, part), jnp.float32),
            pltpu.VMEM(shape, jnp.bfloat16),
        ]
        + [pltpu.SemaphoreType.DMA((ways,))] * 4,
        compiler_params=pltpu.CompilerParams(collective_id=call_id, has_side_effects=True),
        name=f"mix_{call_id}",
    )(cut, params[2][:, None], params[3][:, None], params[4], params[5][:, None], params[6], params[7][:, None])
    return out.transpose(1, 0, 2).reshape(rows, cells)


def edge_strips(tile_grid):
    tile_side = tile_grid.shape[-1]
    first_rows = tile_grid[..., :3, :]
    last_rows = tile_grid[..., tile_side - 3 :, :]
    first_cols = jnp.swapaxes(tile_grid[..., :, :3], -1, -2)
    last_cols = jnp.swapaxes(tile_grid[..., :, tile_side - 3 :], -1, -2)
    return jnp.stack([first_rows, last_rows, first_cols, last_cols], axis=-4)


def padded_tile(own_tile, raw_strips, flip):
    tile_side = own_tile.shape[-1]
    band_list = []
    for band_index, (up_by, right_by) in enumerate(BANDS):
        piece_in = raw_strips[band_index]
        if up_by != 0:
            if up_by == 1:
                piece_in = jnp.where(flip, piece_in[:, ::-1, ::-1], piece_in)
            if right_by == -1:
                piece_in = piece_in[:, :, tile_side - 3 :]
            elif right_by == 1:
                piece_in = piece_in[:, :, :3]
        else:
            piece_in = jnp.swapaxes(piece_in, 1, 2)
        band_list.append(piece_in)
    lower_rows = jnp.concatenate([band_list[0], band_list[1], band_list[2]], axis=2)
    middle_rows = jnp.concatenate([band_list[3], own_tile, band_list[4]], axis=2)
    upper_rows = jnp.concatenate([band_list[5], band_list[6], band_list[7]], axis=2)
    return jnp.concatenate([lower_rows, middle_rows, upper_rows], axis=1)


def depthwise(padded, weights, bias_row):
    chan_rows = padded.shape[0]
    padded_side = padded.shape[1]
    tile_side = padded_side - 6
    flat_cells = padded.astype(jnp.float32).reshape(chan_rows, padded_side * padded_side)
    flat_cells = jnp.pad(flat_cells, ((0, 0), (0, 6)))
    span_cells = tile_side * padded_side
    running = jnp.zeros((chan_rows, span_cells), jnp.float32)
    for row_step in range(7):
        for col_step in range(7):
            offset = row_step * padded_side + col_step
            running = (
                running
                + weights[:, row_step * 7 + col_step][:, None] * flat_cells[:, offset : offset + span_cells]
            )
    conv_out = running.reshape(chan_rows, tile_side, padded_side)[:, :, :tile_side] + bias_row[:, None, None]
    return conv_out.astype(jnp.bfloat16)


def pool_cells(tile_grid, weights):
    values = tile_grid.astype(jnp.float32)
    running = weights[:, 0][:, None, None] * values[:, 0::2, 0::2]
    running = running + weights[:, 1][:, None, None] * values[:, 0::2, 1::2]
    running = running + weights[:, 2][:, None, None] * values[:, 1::2, 0::2]
    running = running + weights[:, 3][:, None, None] * values[:, 1::2, 1::2]
    return running.astype(jnp.bfloat16)


def coarse_mask(mask_grid):
    half_side = mask_grid.shape[0] // 2
    return jnp.max(mask_grid.reshape(half_side, 2, half_side, 2), axis=(1, 3))


def join_levels(fine_flat, coarse_flat, weights, cell_mask, tile_side):
    chan_rows = fine_flat.shape[0]
    half_side = tile_side // 2
    coarse_vals = coarse_flat.astype(jnp.float32).reshape(chan_rows, half_side, half_side)
    spread = weights.reshape(chan_rows, 2, 2)
    expanded = coarse_vals[:, :, None, :, None] * spread[:, None, :, None, :]
    expanded = expanded.reshape(chan_rows, tile_side * tile_side)
    return (cell_mask[None, :] * (fine_flat.astype(jnp.float32) + expanded)).astype(jnp.bfloat16)


def level_body(flat_tile, tile_side, params, cell_mask, table, flip, ways, ids):
    chan_rows = flat_tile.shape[0]
    cell_count = tile_side * tile_side
    tile_grid = flat_tile.reshape(chan_rows, tile_side, tile_side)
    strips = edge_strips(tile_grid).reshape(4, chan_rows * 3 * tile_side)
    got = exchange(strips, table, ids[0])
    raw_strips = [got[band].reshape(chan_rows, 3, tile_side) for band in range(8)]
    padded = padded_tile(tile_grid, raw_strips, flip)
    conv_out = depthwise(padded, params[0], params[1]).reshape(chan_rows, cell_count)
    branch = mix(conv_out, params, ways, ids[1]).astype(jnp.float32)
    scale_row = params[8]
    return (
        cell_mask[None, :] * (flat_tile.astype(jnp.float32) + scale_row[:, None] * branch)
    ).astype(jnp.bfloat16)


def per_device(
    ways,
    features,
    land_mask,
    wet_slots,
    device_of,
    depth_weight,
    depth_bias,
    norm_gain,
    norm_bias,
    up_weight,
    up_bias,
    down_weight,
    down_bias,
    layer_scale,
    pool_weight,
    spread_weight,
):
    tile_count = wet_slots.shape[0]
    table, folded = pick_table(wet_slots, device_of, 2 * tile_count // GRID_Y, GRID_Y)
    flip = lax.dynamic_index_in_dim(folded, lax.axis_index("tile"), 0, keepdims=False)
    stacks = (
        depth_weight,
        depth_bias,
        norm_gain,
        norm_bias,
        up_weight,
        up_bias,
        down_weight,
        down_bias,
        layer_scale,
    )
    fine_params = tuple((array[0] for array in stacks))
    coarse_params = tuple((array[1] for array in stacks))
    fine_mask = land_mask[0].astype(jnp.float32)
    fine_out = level_body(features[0], TILE, fine_params, fine_mask, table, flip, ways, (0, 1))
    chan_rows = fine_out.shape[0]
    half_side = TILE // 2
    pooled = pool_cells(fine_out.reshape(chan_rows, TILE, TILE), pool_weight).reshape(
        chan_rows, half_side * half_side
    )
    small_mask = (
        coarse_mask(land_mask[0].reshape(TILE, TILE)).reshape(half_side * half_side).astype(jnp.float32)
    )
    coarse = level_body(pooled, half_side, coarse_params, small_mask, table, flip, ways, (2, 3))
    merged = join_levels(fine_out, coarse, spread_weight, fine_mask, TILE)
    return merged[None]


def solution(mesh):
    placed = (
        P("tile", "chan", None),
        P("tile", None),
        P(),
        P(),
        P(None, "chan", None),
        P(None, "chan"),
        P(),
        P(),
        P(),
        P(),
        P(),
        P(),
        P(None, "chan"),
        P("chan", None),
        P("chan", None),
    )
    return jax.shard_map(
        functools.partial(per_device, mesh.shape["chan"]),
        mesh=mesh,
        in_specs=placed,
        out_specs=P("tile", "chan", None),
        check_vma=False,
    )
```

```python
import functools

import jax
import jax.numpy as jnp
from jax import lax
from jax.experimental import pallas as pl
from jax.experimental.pallas import tpu as pltpu
from jax.sharding import PartitionSpec as P

TILE = 48
GRID_Y = 4
MESH = pl.DeviceIdType.MESH
norm_eps = 1e-06
VMEM_SPEC = pl.BlockSpec(memory_space=pltpu.VMEM)
SMEM_SPEC = pl.BlockSpec(memory_space=pltpu.SMEM)
LANES = 128
F32 = jnp.float32
BF16 = jnp.bfloat16


class Level:
    def __init__(self, side, parts, slots):
        self.side = side
        self.parts = parts
        self.pitch = LANES // parts
        self.rows = side // parts
        self.slots = slots
        self.edge_units = -(-3 // parts)
        self.side_units = -(-self.rows // slots)
        self.units = 2 * self.edge_units + self.side_units


FINE = Level(TILE, 2, 8)
COARSE = Level(TILE // 2, 4, 3)
MIX_ROWS = (6, 2)


def roll(x, shift):
    shift %= LANES
    return x if shift == 0 else pltpu.roll(x, shift, x.ndim - 1)


def source_table(wet_slots, device_of, grid_x, grid_y):
    tile_count = wet_slots.shape[0]
    devices = jnp.arange(tile_count, dtype=jnp.int32)
    slot = jnp.sum(jnp.where(device_of[None, :] == devices[:, None], wet_slots[None, :], 0), axis=1)
    column = (slot % grid_x)[:, None]
    tile_row = (slot // grid_x)[:, None]
    band = lax.broadcasted_iota(jnp.int32, (1, 8), 1)
    up = jnp.where(band < 3, -1, jnp.where(band < 5, 0, 1))
    right = jnp.where(band < 3, band - 1, jnp.where(band < 5, 2 * band - 7, band - 6))
    near_row = tile_row + up
    folded = near_row >= grid_y
    right = jnp.where(folded, -right, right)
    near_column = (column + right) % grid_x
    source_column = jnp.where(folded, grid_x - 1 - near_column, near_column)
    source_row = jnp.where(folded, grid_y - 1, near_row)
    source_slot = jnp.where(near_row < 0, -1, source_row * grid_x + source_column)
    found = jnp.sum(
        jnp.where(source_slot[:, :, None] == wet_slots[None, None, :], device_of[None, None, :] + 1, 0), axis=2
    )
    table = jnp.where(found > 0, found - 1, tile_count)
    at_fold = (tile_row >= grid_y - 1).astype(jnp.int32)
    return jnp.concatenate([table, at_fold], axis=1)


def lane_ids(shape=(1, LANES)):
    return lax.broadcasted_iota(jnp.int32, shape, len(shape) - 1)


def cut_units(level, grid, units, outgoing):
    lane = lane_ids()
    q = lax.rem(lane, level.pitch)
    part = lane // level.pitch
    side, rows, pitch = level.side, level.rows, level.pitch

    def periodic(j):
        own = grid[j]
        own = jnp.where(q < 3, roll(own, -side), own)
        return jnp.where(q >= side + 3, roll(own, side), own)

    for edge in range(2):
        at = 0 if edge == 0 else level.parts - 1
        for unit in range(level.edge_units):
            value = None
            for k in range(3):
                if k // level.parts != unit:
                    continue
                row = roll(periodic((3 if edge == 0 else rows) + k), (k % level.parts - at) * pitch)
                value = row if value is None else jnp.where(part == k % level.parts, row, value)
            units[edge * level.edge_units + unit] = value.astype(BF16)
    for unit in range(level.side_units):
        value = None
        for slot in range(level.slots):
            j = unit * level.slots + slot
            if j >= rows:
                continue
            own = grid[3 + j]
            both = jnp.where(q < 6 * slot + 3, roll(own, 6 * slot - 3), roll(own, 6 * slot + 3 - side))
            value = both if value is None else jnp.where(q < 6 * slot, value, both)
        units[2 * level.edge_units + unit] = value.astype(BF16)
    pairs = outgoing.shape[0]
    for unit in range(level.units):
        for p in range(pairs):
            outgoing[p, unit] = units[unit, 2 * p : 2 * p + 2, :]


def route(level, tiles, table_ref, outgoing, held, picked, got, send_a, recv_a, send_b, recv_b):
    me = lax.axis_index("tile")
    pieces = outgoing.shape[0]
    piece = (me * pieces + tiles - 1) // tiles
    holds = jnp.logical_and(piece < pieces, (piece * tiles) // pieces == me)
    units, edge = level.units, level.edge_units

    @pl.loop(0, pieces)
    def _(p):
        target = (p * tiles) // pieces

        @pl.when(target != me)
        def _():
            pltpu.make_async_remote_copy(
                src_ref=outgoing.at[p],
                dst_ref=held.at[pl.ds(me * units, units)],
                send_sem=send_a,
                recv_sem=recv_a,
                device_id={"tile": target},
                device_id_type=MESH,
            ).start()

    @pl.when(holds)
    def _():
        held[pl.ds(tiles * units, units)] = jnp.zeros((units, 2, LANES), BF16)
        held[pl.ds(me * units, units)] = outgoing[piece]
        everything = held.at[pl.ds(0, (tiles - 1) * units)]
        pltpu.make_async_copy(everything, everything, recv_a).wait()
        q = lax.rem(lane_ids((2, LANES)), level.pitch)
        left_lanes = q < 3
        own_lanes = q < level.side + 3
        first_lanes = lax.rem(q, 6) < 3

        @pl.loop(0, tiles)
        def _(k):
            target = lax.rem(me + k, tiles)
            base = [table_ref[target * 9 + band] * units for band in range(8)]
            above = table_ref[target * 9 + 8] * edge
            for unit in range(edge):
                for first, offset, place in ((0, edge + unit, unit), (5, above + unit, edge + unit)):
                    left = held[base[first] + offset].astype(F32)
                    own = held[base[first + 1] + offset].astype(F32)
                    right = held[base[first + 2] + offset].astype(F32)
                    row = jnp.where(left_lanes, left, jnp.where(own_lanes, own, right))
                    picked[target, place] = row.astype(BF16)
            for unit in range(2 * edge, units):
                left = held[base[3] + unit].astype(F32)
                right = held[base[4] + unit].astype(F32)
                picked[target, unit] = jnp.where(first_lanes, right, left).astype(BF16)

            @pl.when(k > 0)
            def _():
                pltpu.make_async_remote_copy(
                    src_ref=picked.at[target],
                    dst_ref=got.at[piece],
                    send_sem=send_b,
                    recv_sem=recv_b,
                    device_id={"tile": target},
                    device_id_type=MESH,
                ).start()

        got[piece] = picked[me]
        others = outgoing.at[pl.ds(0, pieces - 1)]
        pltpu.make_async_copy(others, others, send_a).wait()
        arrived = got.at[pl.ds(0, pieces - 1)]
        pltpu.make_async_copy(arrived, arrived, recv_b).wait()
        gone = picked.at[pl.ds(0, tiles - 1)]
        pltpu.make_async_copy(gone, gone, send_b).wait()

    @pl.when(jnp.logical_not(holds))
    def _():
        pltpu.make_async_copy(outgoing, outgoing, send_a).wait()
        pltpu.make_async_copy(got, got, recv_b).wait()


def set_halo(level, grid, units, got, fold):
    pairs = got.shape[0]
    for unit in range(level.units):
        for p in range(pairs):
            units[unit, 2 * p : 2 * p + 2, :] = got[p, unit]
    lane = lane_ids()
    q = lax.rem(lane, level.pitch)
    side, rows, pitch, edge = level.side, level.rows, level.pitch, level.edge_units
    for unit in range(level.side_units):
        value = units[2 * edge + unit].astype(F32)
        for slot in range(level.slots):
            j = unit * level.slots + slot
            if j >= rows:
                continue
            own = jnp.where(q < 3, roll(value, -6 * slot - 3), grid[3 + j])
            grid[3 + j] = jnp.where(q < side + 3, own, roll(value, side + 3 - 6 * slot))
    backwards = (
        lax.broadcasted_iota(jnp.int32, (LANES, LANES), 0) + lax.broadcasted_iota(jnp.int32, (LANES, LANES), 1)
        == side + 5
    ).astype(BF16)
    above = []
    mirrored = []
    for k in range(3):
        below = roll(units[k // level.parts].astype(F32), -(k % level.parts) * pitch)
        grid[k] = jnp.where(lane < pitch, below, roll(grid[rows + k], pitch))
        row = roll(units[edge + k // level.parts].astype(F32), -(k % level.parts) * pitch)
        above.append(row)
        mirrored.append(jnp.dot(row.astype(BF16), backwards, preferred_element_type=F32))
    for k in range(3):
        top = jnp.where(fold > 0.5, mirrored[2 - k], above[k])
        top = roll(top, LANES - pitch)
        grid[rows + 3 + k] = jnp.where(lane >= LANES - pitch, top, roll(grid[3 + k], -pitch))


def depthwise(level, grid, cols_ref, first, bias_at, conv):
    rows = level.rows
    groups = grid.shape[1] // 8

    @pl.loop(0, groups)
    def _(g):
        at = pl.ds(pl.multiple_of(g * 8, 8), 8)
        cols = cols_ref[at, :]
        total = [jnp.broadcast_to(cols[:, bias_at : bias_at + 1], (8, LANES))] * rows
        for b in range(7):
            weights = [
                jnp.broadcast_to(cols[:, first + 7 * a + b : first + 7 * a + b + 1], (8, LANES)) for a in range(7)
            ]
            for j in range(rows + 6):
                shifted = roll(grid[j, at, :], -b)
                for a in range(7):
                    if 0 <= j - a < rows:
                        total[j - a] = total[j - a] + weights[a] * shifted
        for j in range(rows):
            conv[j, at, :] = total[j]


def swap(ways, count, source, target, send, recv):
    me = lax.axis_index("chan")
    copies = []
    for k in range(1, ways):
        peer = lax.rem(me + k, ways)
        copy = pltpu.make_async_remote_copy(
            src_ref=source.at[peer],
            dst_ref=target.at[me],
            send_sem=send.at[k],
            recv_sem=recv.at[k],
            device_id={"chan": peer},
            device_id_type=MESH,
        )
        copy.start()
        copies.append(copy)
    target[me] = source[me]
    for copy in copies:
        copy.wait()


def mix(lev, every, tall_ref, up_ref, upb_ref, down_ref, branch):
    ways, count, chans, _ = every.shape
    hidden_size = up_ref.shape[1]
    step = 256

    @pl.loop(0, count // 2)
    def _(i):
        sides = []
        for jj in range(2):
            values = every[:, 2 * i + jj].astype(F32).reshape(ways * chans, LANES)
            mean = jnp.sum(values, axis=0, keepdims=True) * (1.0 / (ways * chans))
            centred = values - mean
            spread = jnp.sum(centred * centred, axis=0, keepdims=True) * (1.0 / (ways * chans))
            scaled = centred * lax.rsqrt(spread + norm_eps)
            sides.append((scaled * tall_ref[:, lev : lev + 1] + tall_ref[:, 2 + lev : 3 + lev]).astype(BF16))
        normed = jnp.concatenate(sides, axis=1)
        total = jnp.broadcast_to(tall_ref[:, 4 + lev : 5 + lev], (ways * chans, 2 * LANES))
        for h in range(hidden_size // step):
            at = slice(h * step, (h + 1) * step)
            hidden = jnp.dot(up_ref[lev, at, :], normed, preferred_element_type=F32) + upb_ref[at, lev : lev + 1]
            hidden = 0.5 * hidden * (1.0 + lax.erf(hidden * (0.5**0.5)))
            total = total + jnp.dot(down_ref[lev, :, at], hidden.astype(BF16), preferred_element_type=F32)
        for jj in range(2):
            half = total[:, jj * LANES : (jj + 1) * LANES]
            branch[:, 2 * i + jj] = half.reshape(ways, chans, LANES).astype(BF16)


def step_kernel(
    tiles,
    ways,
    table_ref,
    fold_ref,
    features_ref,
    mask_ref,
    mask1_ref,
    cols_ref,
    tall_ref,
    up_ref,
    upb_ref,
    down_ref,
    out_ref,
    grid0,
    grid1,
    units0,
    units1,
    outgoing0,
    outgoing1,
    held0,
    held1,
    picked0,
    picked1,
    got0,
    got1,
    conv,
    sent0,
    sent1,
    every0,
    every1,
    branch0,
    branch1,
    back0,
    back1,
    fine,
    flat,
    sems,
    swaps,
):
    me = lax.axis_index("tile")
    chan = lax.axis_index("chan")
    pieces = outgoing0.shape[0]
    piece = (me * pieces + tiles - 1) // tiles
    holds = jnp.logical_and(piece < pieces, (piece * tiles) // pieces == me)
    barrier = pltpu.get_barrier_semaphore()
    for k in range(1, ways):
        pl.semaphore_signal(barrier, inc=1, device_id={"chan": lax.rem(chan + k, ways)}, device_id_type=MESH)

    @pl.when(holds)
    def _():
        @pl.loop(1, tiles)
        def _(k):
            pl.semaphore_signal(barrier, inc=1, device_id={"tile": lax.rem(me + k, tiles)}, device_id_type=MESH)

    @pl.when(jnp.logical_not(holds))
    def _():
        @pl.loop(0, pieces)
        def _(p):
            pl.semaphore_signal(barrier, inc=1, device_id={"tile": (p * tiles) // pieces}, device_id_type=MESH)

    lane = lane_ids()
    half = TILE * TILE // 2
    flat[...] = features_ref[...].astype(F32)
    for j in range(FINE.rows):
        grid0[3 + j] = jnp.zeros(grid0.shape[1:], F32)
        grid0[3 + j, :, 3 : 3 + TILE] = flat[:, TILE * j : TILE * (j + 1)]
        grid0[3 + j, :, 67 : 67 + TILE] = flat[:, half + TILE * j : half + TILE * (j + 1)]
    cut_units(FINE, grid0, units0, outgoing0)

    @pl.when(holds)
    def _():
        pl.semaphore_wait(barrier, tiles - 1 + ways - 1)

    @pl.when(jnp.logical_not(holds))
    def _():
        pl.semaphore_wait(barrier, pieces + ways - 1)

    fold = fold_ref[...]
    route(FINE, tiles, table_ref, outgoing0, held0, picked0, got0, sems.at[0], sems.at[1], sems.at[2], sems.at[3])
    set_halo(FINE, grid0, units0, got0, fold)
    depthwise(FINE, grid0, cols_ref, 16, 0, conv)
    per = MIX_ROWS[0]
    for j in range(FINE.rows):
        sent0[j // per, j % per] = conv[j].astype(BF16)
    swap(ways, per, sent0, every0, swaps.at[0], swaps.at[1])
    mix(0, every0, tall_ref, up_ref, upb_ref, down_ref, branch0)
    swap(ways, per, branch0, back0, swaps.at[2], swaps.at[3])
    scale = cols_ref[:, 2:3]
    for j in range(FINE.rows):
        value = roll(grid0[3 + j], -3) + scale * back0[j // per, j % per].astype(F32)
        fine[j] = (mask_ref[j] * value).astype(BF16)

    source = lax.broadcasted_iota(jnp.int32, (2 * LANES, LANES), 0)
    target = lax.broadcasted_iota(jnp.int32, (2 * LANES, LANES), 1)
    block = lax.rem(source, LANES)
    wanted = 64 * (block // 64) + 32 * (source // LANES) + lax.rem(block, 64) // 2 + 3
    gather = jnp.logical_and(
        target == wanted, jnp.logical_and(lax.rem(block, 2) == 0, lax.rem(block, 64) < TILE)
    ).astype(BF16)
    pool = [cols_ref[:, 4 + t : 5 + t] for t in range(4)]
    for j in range(COARSE.rows):
        sides = []
        for row in (j, j + COARSE.rows):
            low = fine[2 * row].astype(F32)
            high = fine[2 * row + 1].astype(F32)
            value = pool[0] * low + pool[1] * roll(low, -1) + pool[2] * high + pool[3] * roll(high, -1)
            sides.append(value.astype(BF16))
        grid1[3 + j] = jnp.dot(jnp.concatenate(sides, axis=1), gather, preferred_element_type=F32)
    cut_units(COARSE, grid1, units1, outgoing1)
    route(COARSE, tiles, table_ref, outgoing1, held1, picked1, got1, sems.at[4], sems.at[5], sems.at[6], sems.at[7])
    set_halo(COARSE, grid1, units1, got1, fold)
    depthwise(COARSE, grid1, cols_ref, 65, 1, conv)
    per = MIX_ROWS[1]
    for j in range(ways * per):
        if j < COARSE.rows:
            sent1[j // per, j % per] = conv[j].astype(BF16)
        else:
            sent1[j // per, j % per] = jnp.zeros(sent1.shape[2:], BF16)
    swap(ways, per, sent1, every1, swaps.at[4], swaps.at[5])
    mix(1, every1, tall_ref, up_ref, upb_ref, down_ref, branch1)
    swap(ways, per, branch1, back1, swaps.at[6], swaps.at[7])
    scale = cols_ref[:, 3:4]
    source = lax.broadcasted_iota(jnp.int32, (LANES, LANES), 0)
    target = lax.broadcasted_iota(jnp.int32, (LANES, LANES), 1)
    odd = lax.rem(lane, 2) == 1
    spread = [jnp.where(odd, cols_ref[:, 9 + 2 * t : 10 + 2 * t], cols_ref[:, 8 + 2 * t : 9 + 2 * t]) for t in range(2)]
    for j in range(COARSE.rows):
        value = roll(grid1[3 + j], -3) + scale * back1[j // per, j % per].astype(F32)
        coarse = (mask1_ref[j] * value).astype(BF16)
        for t in range(2):
            wanted = 64 * (target // 64) + 32 * t + lax.rem(target, 64) // 2
            scatter = jnp.logical_and(source == wanted, lax.rem(target, 64) < TILE).astype(BF16)
            wide = jnp.dot(coarse, scatter, preferred_element_type=F32)
            for row in range(2):
                at = 2 * (j + COARSE.rows * t) + row
                value = mask_ref[at] * (fine[at].astype(F32) + spread[row] * wide)
                flat[:, TILE * at : TILE * (at + 1)] = value[:, :TILE]
                flat[:, half + TILE * at : half + TILE * (at + 1)] = value[:, 64 : 64 + TILE]
    out_ref[...] = flat[...].astype(BF16)


def per_device(
    ways,
    features,
    land_mask,
    wet_slots,
    device_of,
    depth_weight,
    depth_bias,
    norm_gain,
    norm_bias,
    up_weight,
    up_bias,
    down_weight,
    down_bias,
    layer_scale,
    pool_weight,
    spread_weight,
):
    tiles = wet_slots.shape[0]
    chans = features.shape[1]
    table = source_table(wet_slots, device_of, 2 * tiles // GRID_Y, GRID_Y)
    fold = lax.dynamic_slice(table, (lax.axis_index("tile"), 8), (1, 1)).astype(F32)
    fold = jnp.broadcast_to(fold, (1, LANES))
    cells = land_mask[0].astype(F32).reshape(2, 24, TILE)
    mask = jnp.pad(cells, ((0, 0), (0, 0), (0, 16))).transpose(1, 0, 2).reshape(24, 1, LANES)
    small = jnp.max(land_mask[0].reshape(24, 2, 24, 2), axis=(1, 3)).astype(F32).reshape(4, 6, 24)
    mask1 = jnp.pad(small, ((0, 0), (0, 0), (0, 8))).transpose(1, 0, 2).reshape(6, 1, LANES)
    cols = jnp.concatenate(
        [
            depth_bias.T,
            layer_scale.T,
            pool_weight,
            spread_weight,
            jnp.zeros((chans, 4), F32),
            depth_weight[0],
            depth_weight[1],
            jnp.zeros((chans, 14), F32),
        ],
        axis=1,
    )
    tall = jnp.concatenate([norm_gain, norm_bias, down_bias, jnp.zeros((2, norm_gain.shape[1]), F32)], axis=0).T
    pairs = chans // 2
    scratch = [
        pltpu.VMEM((FINE.rows + 6, chans, LANES), F32),
        pltpu.VMEM((COARSE.rows + 6, chans, LANES), F32),
    ]
    scratch += [pltpu.VMEM((level.units, chans, LANES), BF16) for level in (FINE, COARSE)]
    scratch += [pltpu.VMEM((pairs, level.units, 2, LANES), BF16) for level in (FINE, COARSE)]
    scratch += [pltpu.VMEM(((tiles + 1) * level.units, 2, LANES), BF16) for level in (FINE, COARSE)]
    scratch += [pltpu.VMEM((tiles, level.units, 2, LANES), BF16) for level in (FINE, COARSE)]
    scratch += [pltpu.VMEM((pairs, level.units, 2, LANES), BF16) for level in (FINE, COARSE)]
    scratch += [pltpu.VMEM((FINE.rows, chans, LANES), F32)]
    scratch += [pltpu.VMEM((ways, per, chans, LANES), BF16) for _ in range(4) for per in MIX_ROWS]
    scratch += [pltpu.VMEM((FINE.rows, chans, LANES), BF16), pltpu.VMEM((chans, TILE * TILE), F32)]
    scratch += [pltpu.SemaphoreType.DMA((8,)), pltpu.SemaphoreType.DMA((8, ways))]
    out = pl.pallas_call(
        functools.partial(step_kernel, tiles, ways),
        out_shape=jax.ShapeDtypeStruct(features.shape[1:], BF16),
        in_specs=[SMEM_SPEC] + [VMEM_SPEC] * 9,
        out_specs=VMEM_SPEC,
        scratch_shapes=scratch,
        compiler_params=pltpu.CompilerParams(
            collective_id=0, has_side_effects=True, vmem_limit_bytes=48 * 1024 * 1024
        ),
        name="ocean_step",
    )(table.reshape(-1), fold, features[0], mask, mask1, cols, tall, up_weight, up_bias.T, down_weight)
    return out[None]


def solution(mesh):
    placed = (
        P("tile", "chan", None),
        P("tile", None),
        P(),
        P(),
        P(None, "chan", None),
        P(None, "chan"),
        P(),
        P(),
        P(),
        P(),
        P(),
        P(),
        P(None, "chan"),
        P("chan", None),
        P("chan", None),
    )
    return jax.shard_map(
        functools.partial(per_device, mesh.shape["chan"]),
        mesh=mesh,
        in_specs=placed,
        out_specs=P("tile", "chan", None),
        check_vma=False,
    )
```

```python
import functools

import jax
import jax.numpy as jnp
from jax import lax
from jax.experimental import pallas as pl
from jax.experimental.pallas import tpu as pltpu
from jax.sharding import PartitionSpec as P

TILE = 48
GRID_Y = 4
MESH = pl.DeviceIdType.MESH
norm_eps = 1e-06
VMEM_SPEC = pl.BlockSpec(memory_space=pltpu.VMEM)
SMEM_SPEC = pl.BlockSpec(memory_space=pltpu.SMEM)
LANES = 128
F32 = jnp.float32
BF16 = jnp.bfloat16


class Level:
    def __init__(self, side, parts, slots):
        self.side = side
        self.parts = parts
        self.pitch = LANES // parts
        self.rows = side // parts
        self.slots = slots
        self.edge_units = -(-3 // parts)
        self.side_units = -(-self.rows // slots)
        self.units = max(2 * self.edge_units, self.side_units)


FINE = Level(TILE, 2, 8)
COARSE = Level(TILE // 2, 4, 3)
MIX_ROWS = (6, 2)


def roll(x, shift):
    shift %= LANES
    return x if shift == 0 else pltpu.roll(x, shift, x.ndim - 1)


def source_table(grid_x, grid_y, wet_ref, device_of_ref, table_ref):
    tiles = wet_ref.shape[1]
    wet = wet_ref[...]
    held_by = device_of_ref[...]
    device = lax.broadcasted_iota(jnp.int32, (tiles, tiles), 0)
    slot = jnp.sum(jnp.where(held_by == device, wet, 0), axis=1, keepdims=True)
    column = lax.rem(slot, grid_x)
    tile_row = lax.div(slot, grid_x)
    band = lax.broadcasted_iota(jnp.int32, (tiles, LANES), 1)
    up = jnp.where(band < 3, -1, jnp.where(band < 5, 0, 1))
    right = jnp.where(band < 3, band - 1, jnp.where(band < 5, 2 * band - 7, band - 6))
    near_row = tile_row + up
    folded = near_row >= grid_y
    right = jnp.where(folded, -right, right)
    near_column = lax.rem(column + right + grid_x, grid_x)
    source_column = jnp.where(folded, grid_x - 1 - near_column, near_column)
    source_row = jnp.where(folded, grid_y - 1, near_row)
    source_slot = jnp.where(near_row < 0, -1, source_row * grid_x + source_column)
    table = jnp.where(tile_row >= grid_y - 1, 1, jnp.zeros((tiles, LANES), jnp.int32))
    fold = jnp.where(device[:, :1] == lax.axis_index("tile"), table, 0)
    fold = jnp.sum(fold.astype(F32), axis=0, keepdims=True)
    for b in range(8):
        here = source_slot[:, b : b + 1] == wet
        found = jnp.sum(jnp.where(here, held_by + 1, 0), axis=1, keepdims=True)
        found = jnp.where(found > 0, found - 1, tiles)
        table = jnp.where(band == b, found, table)
    table_ref[...] = table
    return fold


def lane_ids(shape=(1, LANES)):
    return lax.broadcasted_iota(jnp.int32, shape, len(shape) - 1)


def cut_units(level, grid, units, outgoing):
    lane = lane_ids()
    q = lax.rem(lane, level.pitch)
    part = lane // level.pitch
    side, rows, pitch = level.side, level.rows, level.pitch

    def periodic(j):
        own = grid[j]
        own = jnp.where(q < 3, roll(own, -side), own)
        return jnp.where(q >= side + 3, roll(own, side), own)

    for edge in range(2):
        at = 0 if edge == 0 else level.parts - 1
        for unit in range(level.edge_units):
            value = None
            for k in range(3):
                if k // level.parts != unit:
                    continue
                row = roll(periodic((3 if edge == 0 else rows) + k), (k % level.parts - at) * pitch)
                value = row if value is None else jnp.where(part == k % level.parts, row, value)
            units[0, edge * level.edge_units + unit] = value.astype(BF16)
    for unit in range(level.side_units):
        value = None
        for slot in range(level.slots):
            j = unit * level.slots + slot
            if j >= rows:
                continue
            own = grid[3 + j]
            both = jnp.where(q < 6 * slot + 3, roll(own, 6 * slot - 3), roll(own, 6 * slot + 3 - side))
            value = both if value is None else jnp.where(q < 6 * slot, value, both)
        units[1, unit] = value.astype(BF16)
    for role in range(2):
        for unit in range((2 * level.edge_units, level.side_units)[role]):
            for p in range(outgoing.shape[0] // 2):
                outgoing[2 * p + role, unit] = units[role, unit, 2 * p : 2 * p + 2, :]


def scatter_strips(level, tiles, outgoing, held, send_a, recv_a):
    me = lax.axis_index("tile")
    pieces = outgoing.shape[0]
    units = level.units

    @pl.loop(0, pieces)
    def _(p):
        target = (p * tiles) // pieces

        @pl.when(target != me)
        def _():
            pltpu.make_async_remote_copy(
                src_ref=outgoing.at[p],
                dst_ref=held.at[pl.ds(me * units, units)],
                send_sem=send_a,
                recv_sem=recv_a,
                device_id={"tile": target},
                device_id_type=MESH,
            ).start()


def route(level, tiles, table_ref, outgoing, held, picked, got, send_a, recv_a, send_b, recv_b):
    me = lax.axis_index("tile")
    pieces = outgoing.shape[0]
    piece = (me * pieces + tiles - 1) // tiles
    holds = jnp.logical_and(piece < pieces, (piece * tiles) // pieces == me)
    units, edge = level.units, level.edge_units

    def send(target, k):
        @pl.when(k > 0)
        def _():
            pltpu.make_async_remote_copy(
                src_ref=picked.at[target],
                dst_ref=got.at[piece],
                send_sem=send_b,
                recv_sem=recv_b,
                device_id={"tile": target},
                device_id_type=MESH,
            ).start()

    @pl.when(holds)
    def _():
        held[pl.ds(tiles * units, units)] = jnp.zeros((units, 2, LANES), BF16)
        held[pl.ds(me * units, units)] = outgoing[piece]
        everything = held.at[pl.ds(0, (tiles - 1) * units)]
        pltpu.make_async_copy(everything, everything, recv_a).wait()
        q = lax.rem(lane_ids((2, LANES)), level.pitch)
        left_lanes = q < 3
        own_lanes = q < level.side + 3
        first_lanes = lax.rem(q, 6) < 3

        @pl.when(lax.rem(piece, 2) == 0)
        def _():
            @pl.loop(0, tiles)
            def _(k):
                target = lax.rem(me + k, tiles)
                below = [table_ref[target, band] * units + edge for band in range(3)]
                fold = table_ref[target, 8] * edge
                above = [table_ref[target, band] * units + fold for band in range(5, 8)]
                for unit in range(edge):
                    for base, place in ((below, unit), (above, edge + unit)):
                        left = held[base[0] + unit].astype(F32)
                        own = held[base[1] + unit].astype(F32)
                        right = held[base[2] + unit].astype(F32)
                        row = jnp.where(left_lanes, left, jnp.where(own_lanes, own, right))
                        picked[target, place] = row.astype(BF16)
                send(target, k)

        @pl.when(lax.rem(piece, 2) == 1)
        def _():
            @pl.loop(0, tiles)
            def _(k):
                target = lax.rem(me + k, tiles)
                at_left = table_ref[target, 3] * units
                at_right = table_ref[target, 4] * units
                for unit in range(level.side_units):
                    left = held[at_left + unit].astype(F32)
                    right = held[at_right + unit].astype(F32)
                    picked[target, unit] = jnp.where(first_lanes, right, left).astype(BF16)
                send(target, k)

        got[piece] = picked[me]
        others = outgoing.at[pl.ds(0, pieces - 1)]
        pltpu.make_async_copy(others, others, send_a).wait()
        arrived = got.at[pl.ds(0, pieces - 1)]
        pltpu.make_async_copy(arrived, arrived, recv_b).wait()
        gone = picked.at[pl.ds(0, tiles - 1)]
        pltpu.make_async_copy(gone, gone, send_b).wait()

    @pl.when(jnp.logical_not(holds))
    def _():
        pltpu.make_async_copy(outgoing, outgoing, send_a).wait()
        pltpu.make_async_copy(got, got, recv_b).wait()


def set_halo(level, grid, units, got, fold):
    for role in range(2):
        for unit in range((2 * level.edge_units, level.side_units)[role]):
            for p in range(got.shape[0] // 2):
                units[role, unit, 2 * p : 2 * p + 2, :] = got[2 * p + role, unit]
    lane = lane_ids()
    q = lax.rem(lane, level.pitch)
    side, rows, pitch, edge = level.side, level.rows, level.pitch, level.edge_units
    for unit in range(level.side_units):
        value = units[1, unit].astype(F32)
        for slot in range(level.slots):
            j = unit * level.slots + slot
            if j >= rows:
                continue
            own = jnp.where(q < 3, roll(value, -6 * slot - 3), grid[3 + j])
            grid[3 + j] = jnp.where(q < side + 3, own, roll(value, side + 3 - 6 * slot))
    backwards = (
        lax.broadcasted_iota(jnp.int32, (LANES, LANES), 0) + lax.broadcasted_iota(jnp.int32, (LANES, LANES), 1)
        == side + 5
    ).astype(BF16)
    above = []
    mirrored = []
    for k in range(3):
        below = roll(units[0, k // level.parts].astype(F32), -(k % level.parts) * pitch)
        grid[k] = jnp.where(lane < pitch, below, roll(grid[rows + k], pitch))
        row = roll(units[0, edge + k // level.parts].astype(F32), -(k % level.parts) * pitch)
        above.append(row)
        mirrored.append(jnp.dot(row.astype(BF16), backwards, preferred_element_type=F32))
    for k in range(3):
        top = jnp.where(fold > 0.5, mirrored[2 - k], above[k])
        top = roll(top, LANES - pitch)
        grid[rows + 3 + k] = jnp.where(lane >= LANES - pitch, top, roll(grid[3 + k], -pitch))


def start_swap(ways, source, target, send, recv, window):
    me = lax.axis_index("chan")
    for k in range(1, ways):
        peer = lax.rem(me + k, ways)
        pltpu.make_async_remote_copy(
            src_ref=source.at[(peer,) + window],
            dst_ref=target.at[(me,) + window],
            send_sem=send.at[k],
            recv_sem=recv.at[k],
            device_id={"chan": peer},
            device_id_type=MESH,
        ).start()


def finish_swap(ways, source, target, send, recv):
    me = lax.axis_index("chan")
    target[me] = source[me]
    for k in range(1, ways):
        block = source.at[k]
        pltpu.make_async_copy(block, block, send.at[k]).wait()
        pltpu.make_async_copy(block, block, recv.at[k]).wait()


def depthwise(level, lev, grid, taps_ref, cols, conv, sent, every, send, recv):
    rows = level.rows
    ways, per = sent.shape[:2]
    wide = 16
    for j in range(rows, ways * per):
        sent[j // per, j % per] = jnp.zeros(sent.shape[2:], BF16)

    @pl.loop(0, grid.shape[1] // wide)
    def _(g):
        both = pl.ds(pl.multiple_of(g * wide, wide), wide)
        for part in range(2):
            at = pl.ds(pl.multiple_of(g * wide + part * 8, 8), 8)
            taps = taps_ref[lev, at, :]
            total = [jnp.broadcast_to(cols[at, lev : lev + 1], (8, LANES))] * rows
            for b in range(7):
                weights = [jnp.broadcast_to(taps[:, 7 * a + b : 7 * a + b + 1], (8, LANES)) for a in range(7)]
                for j in range(rows + 6):
                    shifted = roll(grid[j, at, :], -b)
                    for a in range(7):
                        if 0 <= j - a < rows:
                            total[j - a] = total[j - a] + weights[a] * shifted
            for j in range(rows):
                conv[j, at, :] = total[j]
        for j in range(rows):
            sent[j // per, j % per, both, :] = conv[j, both, :].astype(BF16)
        start_swap(ways, sent, every, send, recv, (slice(None), both))

    finish_swap(ways, sent, every, send, recv)


def mix(lev, every, tall_ref, up_ref, upb_ref, down_ref, branch, back, send, recv):
    ways, count, chans, _ = every.shape
    hidden_size = up_ref.shape[1]
    step = 256

    @pl.loop(0, count // 2)
    def _(i):
        sides = []
        for jj in range(2):
            values = every[:, 2 * i + jj].astype(F32).reshape(ways * chans, LANES)
            mean = jnp.sum(values, axis=0, keepdims=True) * (1.0 / (ways * chans))
            centred = values - mean
            spread = jnp.sum(centred * centred, axis=0, keepdims=True) * (1.0 / (ways * chans))
            scaled = centred * lax.rsqrt(spread + norm_eps)
            sides.append((scaled * tall_ref[:, lev : lev + 1] + tall_ref[:, 2 + lev : 3 + lev]).astype(BF16))
        normed = jnp.concatenate(sides, axis=1)
        total = jnp.broadcast_to(tall_ref[:, 4 + lev : 5 + lev], (ways * chans, 2 * LANES))
        for h in range(hidden_size // step):
            at = slice(h * step, (h + 1) * step)
            hidden = jnp.dot(up_ref[lev, at, :], normed, preferred_element_type=F32) + upb_ref[at, lev : lev + 1]
            hidden = 0.5 * hidden * (1.0 + lax.erf(hidden * (0.5**0.5)))
            total = total + jnp.dot(down_ref[lev, :, at], hidden.astype(BF16), preferred_element_type=F32)
        for jj in range(2):
            half = total[:, jj * LANES : (jj + 1) * LANES]
            branch[:, 2 * i + jj] = half.reshape(ways, chans, LANES).astype(BF16)
        start_swap(ways, branch, back, send, recv, (pl.ds(2 * i, 2),))

    finish_swap(ways, branch, back, send, recv)


def columns(block):
    return jnp.transpose(block)


def step_kernel(
    tiles,
    ways,
    wet_ref,
    device_of_ref,
    features_ref,
    land_ref,
    taps_ref,
    bias_ref,
    gain_ref,
    shift_ref,
    up_ref,
    up_bias_ref,
    down_ref,
    down_bias_ref,
    scale_ref,
    pool_ref,
    spread_ref,
    out_ref,
    table_v,
    table_s,
    rows_a,
    rows_b,
    rows_c,
    cols,
    tall,
    upb,
    mask,
    mask1,
    gather,
    grid0,
    grid1,
    units0,
    units1,
    outgoing0,
    outgoing1,
    held0,
    held1,
    picked0,
    picked1,
    got0,
    got1,
    conv,
    sent0,
    sent1,
    every0,
    every1,
    branch0,
    branch1,
    back0,
    back1,
    fine,
    flat,
    sems,
    swaps,
):
    me = lax.axis_index("tile")
    chan = lax.axis_index("chan")
    pieces = outgoing0.shape[0]
    chans = grid0.shape[1]
    piece = (me * pieces + tiles - 1) // tiles
    holds = jnp.logical_and(piece < pieces, (piece * tiles) // pieces == me)
    barrier = pltpu.get_barrier_semaphore()

    @pl.when(holds)
    def _():
        @pl.loop(1, tiles)
        def _(k):
            pl.semaphore_signal(barrier, inc=1, device_id={"tile": lax.rem(me + k, tiles)}, device_id_type=MESH)

    @pl.when(jnp.logical_not(holds))
    def _():
        @pl.loop(0, pieces)
        def _(p):
            pl.semaphore_signal(barrier, inc=1, device_id={"tile": (p * tiles) // pieces}, device_id_type=MESH)

    for k in range(1, ways):
        pl.semaphore_signal(barrier, inc=1, device_id={"chan": lax.rem(chan + k, ways)}, device_id_type=MESH)

    lane = lane_ids()
    half = TILE * TILE // 2
    flat[...] = features_ref[...].astype(F32)
    for j in range(FINE.rows):
        grid0[3 + j] = jnp.zeros(grid0.shape[1:], F32)
        grid0[3 + j, :, 3 : 3 + TILE] = flat[:, TILE * j : TILE * (j + 1)]
        grid0[3 + j, :, 67 : 67 + TILE] = flat[:, half + TILE * j : half + TILE * (j + 1)]
    for outgoing in (outgoing0, outgoing1):
        outgoing[...] = jnp.zeros(outgoing.shape, BF16)
    cut_units(FINE, grid0, units0, outgoing0)

    @pl.when(holds)
    def _():
        pl.semaphore_wait(barrier, tiles - 1 + ways - 1)

    @pl.when(jnp.logical_not(holds))
    def _():
        pl.semaphore_wait(barrier, pieces + ways - 1)

    scatter_strips(FINE, tiles, outgoing0, held0, sems.at[0], sems.at[1])

    fold = source_table(2 * tiles // GRID_Y, GRID_Y, wet_ref, device_of_ref, table_v)
    table_copy = pltpu.make_async_copy(table_v, table_s, sems.at[8])
    table_copy.start()
    rows_a[...] = jnp.zeros(rows_a.shape, F32)
    for at, ref in ((0, bias_ref), (2, scale_ref), (4, pool_ref), (8, spread_ref)):
        rows_a[at : at + ref.shape[0], :chans] = ref[...]
    cols[...] = columns(rows_a[...])[:chans]
    rows_b[...] = jnp.zeros(rows_b.shape, F32)
    for at, ref in ((0, gain_ref), (2, shift_ref), (4, down_bias_ref)):
        rows_b[at : at + 2, : ways * chans] = ref[...]
    tall[...] = columns(rows_b[...])[: ways * chans]
    rows_c[...] = jnp.zeros(rows_c.shape, F32)
    rows_c[0:2, :] = up_bias_ref[...]
    upb[...] = columns(rows_c[...])
    flat[0:1, :] = land_ref[...].astype(F32)
    for j in range(FINE.rows):
        mask[j] = jnp.zeros((1, LANES), F32)
        mask[j, :, :TILE] = flat[0:1, TILE * j : TILE * (j + 1)]
        mask[j, :, 64 : 64 + TILE] = flat[0:1, half + TILE * j : half + TILE * (j + 1)]
    source = lax.broadcasted_iota(jnp.int32, (2 * LANES, LANES), 0)
    target = lax.broadcasted_iota(jnp.int32, (2 * LANES, LANES), 1)
    block = lax.rem(source, LANES)
    wanted = 64 * (block // 64) + 32 * (source // LANES) + lax.rem(block, 64) // 2 + 3
    gather[...] = jnp.logical_and(
        target == wanted, jnp.logical_and(lax.rem(block, 2) == 0, lax.rem(block, 64) < TILE)
    ).astype(BF16)
    for j in range(COARSE.rows):
        sides = []
        for row in (j, j + COARSE.rows):
            value = jnp.broadcast_to(jnp.maximum(mask[2 * row], mask[2 * row + 1]), (8, LANES))
            sides.append(jnp.maximum(value, roll(value, -1)).astype(BF16))
        value = jnp.dot(jnp.concatenate(sides, axis=1), gather[...], preferred_element_type=F32)
        mask1[j] = roll(value, -3)[0:1]
    table_copy.wait()

    route(FINE, tiles, table_s, outgoing0, held0, picked0, got0, sems.at[0], sems.at[1], sems.at[2], sems.at[3])
    set_halo(FINE, grid0, units0, got0, fold)
    depthwise(FINE, 0, grid0, taps_ref, cols, conv, sent0, every0, swaps.at[0], swaps.at[1])
    mix(0, every0, tall, up_ref, upb, down_ref, branch0, back0, swaps.at[2], swaps.at[3])
    per = MIX_ROWS[0]
    scale = cols[:, 2:3]
    for j in range(FINE.rows):
        value = roll(grid0[3 + j], -3) + scale * back0[j // per, j % per].astype(F32)
        fine[j] = (mask[j] * value).astype(BF16)
    pool = [cols[:, 4 + t : 5 + t] for t in range(4)]
    for j in range(COARSE.rows):
        sides = []
        for row in (j, j + COARSE.rows):
            low = fine[2 * row].astype(F32)
            high = fine[2 * row + 1].astype(F32)
            value = pool[0] * low + pool[1] * roll(low, -1) + pool[2] * high + pool[3] * roll(high, -1)
            sides.append(value.astype(BF16))
        grid1[3 + j] = jnp.dot(jnp.concatenate(sides, axis=1), gather[...], preferred_element_type=F32)
    cut_units(COARSE, grid1, units1, outgoing1)
    scatter_strips(COARSE, tiles, outgoing1, held1, sems.at[4], sems.at[5])
    route(COARSE, tiles, table_s, outgoing1, held1, picked1, got1, sems.at[4], sems.at[5], sems.at[6], sems.at[7])
    set_halo(COARSE, grid1, units1, got1, fold)
    depthwise(COARSE, 1, grid1, taps_ref, cols, conv, sent1, every1, swaps.at[4], swaps.at[5])
    mix(1, every1, tall, up_ref, upb, down_ref, branch1, back1, swaps.at[6], swaps.at[7])
    per = MIX_ROWS[1]
    scale = cols[:, 3:4]
    source = lax.broadcasted_iota(jnp.int32, (LANES, LANES), 0)
    target = lax.broadcasted_iota(jnp.int32, (LANES, LANES), 1)
    odd = lax.rem(lane, 2) == 1
    spread = [jnp.where(odd, cols[:, 9 + 2 * t : 10 + 2 * t], cols[:, 8 + 2 * t : 9 + 2 * t]) for t in range(2)]
    for j in range(COARSE.rows):
        value = roll(grid1[3 + j], -3) + scale * back1[j // per, j % per].astype(F32)
        coarse = (mask1[j] * value).astype(BF16)
        for t in range(2):
            wanted = 64 * (target // 64) + 32 * t + lax.rem(target, 64) // 2
            scatter = jnp.logical_and(source == wanted, lax.rem(target, 64) < TILE).astype(BF16)
            wide = jnp.dot(coarse, scatter, preferred_element_type=F32)
            for row in range(2):
                at = 2 * (j + COARSE.rows * t) + row
                value = mask[at] * (fine[at].astype(F32) + spread[row] * wide)
                flat[:, TILE * at : TILE * (at + 1)] = value[:, :TILE]
                flat[:, half + TILE * at : half + TILE * (at + 1)] = value[:, 64 : 64 + TILE]
    out_ref[...] = flat[...].astype(BF16)


def per_device(
    ways,
    features,
    land_mask,
    wet_slots,
    device_of,
    depth_weight,
    depth_bias,
    norm_gain,
    norm_bias,
    up_weight,
    up_bias,
    down_weight,
    down_bias,
    layer_scale,
    pool_weight,
    spread_weight,
):
    tiles = wet_slots.shape[0]
    chans = features.shape[1]
    levels = (FINE, COARSE)
    scratch = [
        pltpu.VMEM((tiles, LANES), jnp.int32),
        pltpu.SMEM((tiles, LANES), jnp.int32),
        pltpu.VMEM((16, LANES), F32),
        pltpu.VMEM((8, 2 * LANES), F32),
        pltpu.VMEM((8, up_bias.shape[1]), F32),
        pltpu.VMEM((chans, 16), F32),
        pltpu.VMEM((ways * chans, 8), F32),
        pltpu.VMEM((up_bias.shape[1], 8), F32),
        pltpu.VMEM((FINE.rows, 1, LANES), F32),
        pltpu.VMEM((COARSE.rows, 1, LANES), F32),
        pltpu.VMEM((2 * LANES, LANES), BF16),
        pltpu.VMEM((FINE.rows + 6, chans, LANES), F32),
        pltpu.VMEM((COARSE.rows + 6, chans, LANES), F32),
    ]
    scratch += [pltpu.VMEM((2, level.units, chans, LANES), BF16) for level in levels]
    scratch += [pltpu.VMEM((chans, level.units, 2, LANES), BF16) for level in levels]
    scratch += [pltpu.VMEM(((tiles + 1) * level.units, 2, LANES), BF16) for level in levels]
    scratch += [pltpu.VMEM((tiles, level.units, 2, LANES), BF16) for level in levels]
    scratch += [pltpu.VMEM((chans, level.units, 2, LANES), BF16) for level in levels]
    scratch += [pltpu.VMEM((FINE.rows, chans, LANES), F32)]
    scratch += [pltpu.VMEM((ways, per, chans, LANES), BF16) for _ in range(4) for per in MIX_ROWS]
    scratch += [pltpu.VMEM((FINE.rows, chans, LANES), BF16), pltpu.VMEM((chans, TILE * TILE), F32)]
    scratch += [pltpu.SemaphoreType.DMA((9,)), pltpu.SemaphoreType.DMA((8, ways))]
    out = pl.pallas_call(
        functools.partial(step_kernel, tiles, ways),
        out_shape=jax.ShapeDtypeStruct(features.shape[1:], BF16),
        in_specs=[VMEM_SPEC] * 15,
        out_specs=VMEM_SPEC,
        scratch_shapes=scratch,
        compiler_params=pltpu.CompilerParams(
            collective_id=0, has_side_effects=True, vmem_limit_bytes=48 * 1024 * 1024
        ),
        name="ocean_step",
    )(
        wet_slots[None],
        device_of[None],
        features[0],
        land_mask,
        depth_weight,
        depth_bias,
        norm_gain,
        norm_bias,
        up_weight,
        up_bias,
        down_weight,
        down_bias,
        layer_scale,
        pool_weight.T,
        spread_weight.T,
    )
    return out[None]


def solution(mesh):
    placed = (
        P("tile", "chan", None),
        P("tile", None),
        P(),
        P(),
        P(None, "chan", None),
        P(None, "chan"),
        P(),
        P(),
        P(),
        P(),
        P(),
        P(),
        P(None, "chan"),
        P("chan", None),
        P("chan", None),
    )
    return jax.shard_map(
        functools.partial(per_device, mesh.shape["chan"]),
        mesh=mesh,
        in_specs=placed,
        out_specs=P("tile", "chan", None),
        check_vma=False,
    )
```

```python
import functools

import jax
import jax.numpy as jnp
from jax import lax
from jax.experimental import pallas as pl
from jax.experimental.pallas import tpu as pltpu
from jax.sharding import PartitionSpec as P

TILE = 48
GRID_Y = 4
MESH = pl.DeviceIdType.MESH
norm_eps = 1e-06
VMEM_SPEC = pl.BlockSpec(memory_space=pltpu.VMEM)
SMEM_SPEC = pl.BlockSpec(memory_space=pltpu.SMEM)
LANES = 128
F32 = jnp.float32
BF16 = jnp.bfloat16


class Level:
    def __init__(self, side, parts, slots):
        self.side = side
        self.parts = parts
        self.pitch = LANES // parts
        self.rows = side // parts
        self.slots = slots
        self.edge_units = -(-3 // parts)
        self.side_units = -(-self.rows // slots)
        self.units = max(2 * self.edge_units, self.side_units)


FINE = Level(TILE, 2, 8)
COARSE = Level(TILE // 2, 4, 3)


def roll(x, shift):
    shift %= LANES
    return x if shift == 0 else pltpu.roll(x, shift, x.ndim - 1)


def source_table(grid_x, grid_y, wet_ref, device_of_ref, table_ref):
    tiles = wet_ref.shape[1]
    wet = wet_ref[...]
    held_by = device_of_ref[...]
    device = lax.broadcasted_iota(jnp.int32, (tiles, tiles), 0)
    slot = jnp.sum(jnp.where(held_by == device, wet, 0), axis=1, keepdims=True)
    column = lax.rem(slot, grid_x)
    tile_row = lax.div(slot, grid_x)
    band = lax.broadcasted_iota(jnp.int32, (tiles, LANES), 1)
    up = jnp.where(band < 3, -1, jnp.where(band < 5, 0, 1))
    right = jnp.where(band < 3, band - 1, jnp.where(band < 5, 2 * band - 7, band - 6))
    near_row = tile_row + up
    folded = near_row >= grid_y
    right = jnp.where(folded, -right, right)
    near_column = lax.rem(column + right + grid_x, grid_x)
    source_column = jnp.where(folded, grid_x - 1 - near_column, near_column)
    source_row = jnp.where(folded, grid_y - 1, near_row)
    source_slot = jnp.where(near_row < 0, -1, source_row * grid_x + source_column)
    table = jnp.where(tile_row >= grid_y - 1, 1, jnp.zeros((tiles, LANES), jnp.int32))
    fold = jnp.where(device[:, :1] == lax.axis_index("tile"), table, 0)
    fold = jnp.sum(fold.astype(F32), axis=0, keepdims=True)
    for b in range(8):
        here = source_slot[:, b : b + 1] == wet
        found = jnp.sum(jnp.where(here, held_by + 1, 0), axis=1, keepdims=True)
        found = jnp.where(found > 0, found - 1, tiles)
        table = jnp.where(band == b, found, table)
    table_ref[...] = table
    return fold


def each_other_tile(me, tiles, body):
    layer = 16
    deep = tiles // layer
    mine = me // layer
    low = lax.rem(me, layer)

    @pl.loop(0, deep - 1)
    def _(n):
        half = (n + 1) // 2
        z = lax.rem(mine + deep // 2 + half * (2 * lax.rem(n, 2) - 1) + deep, deep)

        @pl.loop(0, layer // 4)
        def _(i):
            body([z * layer + lax.rem(low + layer // 2 + 4 * i + t, layer) for t in range(4)])

    @pl.loop(0, layer // 4 - 1)
    def _(i):
        body([mine * layer + lax.rem(low + 4 + 4 * i + t, layer) for t in range(4)])

    body([mine * layer + lax.rem(low + t, layer) for t in range(1, 4)])


def each_piece(me, pieces, tiles, body):
    start = (me * pieces) // tiles + pieces // 2

    @pl.loop(0, pieces // 2)
    def _(i):
        body(lax.rem(start + i, pieces))
        body(lax.rem(start + pieces - 1 - i, pieces))


def lane_ids(shape=(1, LANES)):
    return lax.broadcasted_iota(jnp.int32, shape, len(shape) - 1)


def cut_units(level, grid, units, outgoing):
    lane = lane_ids()
    q = lax.rem(lane, level.pitch)
    part = lane // level.pitch
    side, rows, pitch = level.side, level.rows, level.pitch

    def periodic(j):
        own = grid[j]
        own = jnp.where(q < 3, roll(own, -side), own)
        return jnp.where(q >= side + 3, roll(own, side), own)

    for edge in range(2):
        at = 0 if edge == 0 else level.parts - 1
        for unit in range(level.edge_units):
            value = None
            for k in range(3):
                if k // level.parts != unit:
                    continue
                row = roll(periodic((3 if edge == 0 else rows) + k), (k % level.parts - at) * pitch)
                value = row if value is None else jnp.where(part == k % level.parts, row, value)
            units[0, edge * level.edge_units + unit] = value.astype(BF16)
    for unit in range(level.side_units):
        value = None
        for slot in range(level.slots):
            j = unit * level.slots + slot
            if j >= rows:
                continue
            own = grid[3 + j]
            both = jnp.where(q < 6 * slot + 3, roll(own, 6 * slot - 3), roll(own, 6 * slot + 3 - side))
            value = both if value is None else jnp.where(q < 6 * slot, value, both)
        units[1, unit] = value.astype(BF16)
    for role in range(2):
        for unit in range((2 * level.edge_units, level.side_units)[role]):
            for p in range(outgoing.shape[0] // 2):
                outgoing[2 * p + role, unit] = units[role, unit, 2 * p : 2 * p + 2, :]


def scatter_strips(level, tiles, outgoing, held, send_a, recv_a):
    me = lax.axis_index("tile")
    pieces = outgoing.shape[0]
    units = level.units

    def send(p):
        target = (p * tiles) // pieces

        @pl.when(target != me)
        def _():
            pltpu.make_async_remote_copy(
                src_ref=outgoing.at[p],
                dst_ref=held.at[pl.ds(me * units, units)],
                send_sem=send_a,
                recv_sem=recv_a,
                device_id={"tile": target},
                device_id_type=MESH,
            ).start()

    each_piece(me, pieces, tiles, send)


def serve_strips(level, tiles, table_ref, outgoing, held, picked, got, recv_a, send_b, recv_b):
    me = lax.axis_index("tile")
    pieces = outgoing.shape[0]
    piece = (me * pieces + tiles - 1) // tiles
    holds = jnp.logical_and(piece < pieces, (piece * tiles) // pieces == me)
    units, edge = level.units, level.edge_units

    def send(target):
        pltpu.make_async_remote_copy(
            src_ref=picked.at[target],
            dst_ref=got.at[piece],
            send_sem=send_b,
            recv_sem=recv_b,
            device_id={"tile": target},
            device_id_type=MESH,
        ).start()

    @pl.when(holds)
    def _():
        held[pl.ds(tiles * units, units)] = jnp.zeros((units, 2, LANES), BF16)
        held[pl.ds(me * units, units)] = outgoing[piece]
        everything = held.at[pl.ds(0, (tiles - 1) * units)]
        pltpu.make_async_copy(everything, everything, recv_a).wait()
        q = lax.rem(lane_ids((2, LANES)), level.pitch)
        left_lanes = q < 3
        own_lanes = q < level.side + 3
        first_lanes = lax.rem(q, 6) < 3

        @pl.when(lax.rem(piece, 2) == 0)
        def _():
            def pick(target):
                below = [table_ref[target, band] * units + edge for band in range(3)]
                fold = table_ref[target, 8] * edge
                above = [table_ref[target, band] * units + fold for band in range(5, 8)]
                for unit in range(edge):
                    for base, place in ((below, unit), (above, edge + unit)):
                        left = held[base[0] + unit].astype(F32)
                        own = held[base[1] + unit].astype(F32)
                        right = held[base[2] + unit].astype(F32)
                        row = jnp.where(left_lanes, left, jnp.where(own_lanes, own, right))
                        picked[target, place] = row.astype(BF16)

            def pick_and_send(targets):
                for target in targets:
                    pick(target)
                for target in targets:
                    send(target)

            each_other_tile(me, tiles, pick_and_send)
            pick(me)

        @pl.when(lax.rem(piece, 2) == 1)
        def _():
            def pick(target):
                at_left = table_ref[target, 3] * units
                at_right = table_ref[target, 4] * units
                for unit in range(level.side_units):
                    left = held[at_left + unit].astype(F32)
                    right = held[at_right + unit].astype(F32)
                    picked[target, unit] = jnp.where(first_lanes, right, left).astype(BF16)

            def pick_and_send(targets):
                for target in targets:
                    pick(target)
                for target in targets:
                    send(target)

            each_other_tile(me, tiles, pick_and_send)
            pick(me)

        got[piece] = picked[me]

def collect_strips(tiles, outgoing, picked, got, send_a, send_b, recv_b):
    me = lax.axis_index("tile")
    pieces = outgoing.shape[0]
    piece = (me * pieces + tiles - 1) // tiles
    holds = jnp.logical_and(piece < pieces, (piece * tiles) // pieces == me)

    @pl.when(holds)
    def _():
        others = outgoing.at[pl.ds(0, pieces - 1)]
        pltpu.make_async_copy(others, others, send_a).wait()
        arrived = got.at[pl.ds(0, pieces - 1)]
        pltpu.make_async_copy(arrived, arrived, recv_b).wait()
        gone = picked.at[pl.ds(0, tiles - 1)]
        pltpu.make_async_copy(gone, gone, send_b).wait()

    @pl.when(jnp.logical_not(holds))
    def _():
        pltpu.make_async_copy(outgoing, outgoing, send_a).wait()
        pltpu.make_async_copy(got, got, recv_b).wait()


def close_parts(level, grid):
    lane = lane_ids()
    rows, pitch = level.rows, level.pitch
    for k in range(3):
        grid[k] = jnp.where(lane < pitch, 0.0, roll(grid[rows + k], pitch))
        grid[rows + 3 + k] = jnp.where(lane >= LANES - pitch, 0.0, roll(grid[3 + k], -pitch))


def set_rim(level, rim, units, got, fold):
    for role in range(2):
        for unit in range((2 * level.edge_units, level.side_units)[role]):
            for p in range(got.shape[0] // 2):
                units[role, unit, 2 * p : 2 * p + 2, :] = got[2 * p + role, unit]
    lane = lane_ids()
    q = lax.rem(lane, level.pitch)
    side, rows, pitch, edge = level.side, level.rows, level.pitch, level.edge_units
    for unit in range(level.side_units):
        value = units[1, unit].astype(F32)
        for slot in range(level.slots):
            j = unit * level.slots + slot
            if j >= rows:
                continue
            own = jnp.where(q < 3, roll(value, -6 * slot - 3), 0.0)
            rim[3 + j] = jnp.where(q < side + 3, own, roll(value, side + 3 - 6 * slot))
    backwards = (
        lax.broadcasted_iota(jnp.int32, (LANES, LANES), 0) + lax.broadcasted_iota(jnp.int32, (LANES, LANES), 1)
        == side + 5
    ).astype(BF16)
    above = []
    mirrored = []
    for k in range(3):
        below = roll(units[0, k // level.parts].astype(F32), -(k % level.parts) * pitch)
        rim[k] = jnp.where(lane < pitch, below, roll(rim[rows + k], pitch))
        row = roll(units[0, edge + k // level.parts].astype(F32), -(k % level.parts) * pitch)
        above.append(row)
        mirrored.append(jnp.dot(row.astype(BF16), backwards, preferred_element_type=F32))
    for k in range(3):
        top = jnp.where(fold > 0.5, mirrored[2 - k], above[k])
        top = roll(top, LANES - pitch)
        rim[rows + 3 + k] = jnp.where(lane >= LANES - pitch, top, roll(rim[3 + k], -pitch))


def start_swap(ways, source, target, send, recv, window):
    me = lax.axis_index("chan")
    for k in range(1, ways):
        peer = lax.rem(me + k, ways)
        pltpu.make_async_remote_copy(
            src_ref=source.at[(peer,) + window],
            dst_ref=target.at[(me,) + window],
            send_sem=send.at[k],
            recv_sem=recv.at[k],
            device_id={"chan": peer},
            device_id_type=MESH,
        ).start()


def finish_swap(ways, source, target, send, recv):
    me = lax.axis_index("chan")
    target[me] = source[me]
    for k in range(1, ways):
        block = source.at[k]
        pltpu.make_async_copy(block, block, send.at[k]).wait()
        pltpu.make_async_copy(block, block, recv.at[k]).wait()


def start_gather(ways, source, target, send, recv, window):
    me = lax.axis_index("chan")
    for k in range(1, ways):
        pltpu.make_async_remote_copy(
            src_ref=source.at[window],
            dst_ref=target.at[(me,) + window],
            send_sem=send.at[k],
            recv_sem=recv.at[k],
            device_id={"chan": lax.rem(me + k, ways)},
            device_id_type=MESH,
        ).start()


def finish_gather(ways, source, target, send, recv):
    target[lax.axis_index("chan")] = source[...]
    for k in range(1, ways):
        pltpu.make_async_copy(source, source, send.at[k]).wait()
        pltpu.make_async_copy(source, source, recv.at[k]).wait()


def depthwise_inside(level, lev, grid, taps_ref, cols, conv):
    rows = level.rows

    @pl.loop(0, grid.shape[1] // 8)
    def _(g):
        at = pl.ds(pl.multiple_of(g * 8, 8), 8)
        taps = taps_ref[lev, at, :]
        total = [jnp.broadcast_to(cols[at, lev : lev + 1], (8, LANES))] * rows
        for b in range(7):
            weights = [jnp.broadcast_to(taps[:, 7 * a + b : 7 * a + b + 1], (8, LANES)) for a in range(7)]
            for j in range(rows + 6):
                shifted = roll(grid[j, at, :], -b)
                for a in range(7):
                    if 0 <= j - a < rows:
                        total[j - a] = total[j - a] + weights[a] * shifted
        for j in range(rows):
            conv[j, at, :] = total[j]


def depthwise_rim(level, lev, ways, rim, taps_ref, conv, sent, every, send, recv):
    rows = level.rows
    split = len(sent.shape) == 4
    per = sent.shape[1] if split else rows
    wide = 16
    near = lax.rem(lane_ids((8, LANES)), level.pitch) < 8

    @pl.loop(0, rim.shape[1] // wide)
    def _(g):
        both = pl.ds(pl.multiple_of(g * wide, wide), wide)
        for part in range(2):
            at = pl.ds(pl.multiple_of(g * wide + part * 8, 8), 8)
            taps = taps_ref[lev, at, :]
            total = [conv[j, at, :] for j in range(rows)]

            def tap(a, b):
                return jnp.broadcast_to(taps[:, 7 * a + b : 7 * a + b + 1], (8, LANES))

            for b in range(7):
                weights = [tap(a, b) for a in range(7)]
                for j in (0, 1, 2, rows + 3, rows + 4, rows + 5):
                    shifted = roll(rim[j, at, :], -b)
                    for a in range(7):
                        if 0 <= j - a < rows:
                            total[j - a] = total[j - a] + weights[a] * shifted
            for b in range(3):
                weights = [jnp.where(near, tap(a, b), tap(a, b + 4)) for a in range(7)]
                for j in range(3, rows + 3):
                    cells = rim[j, at, :]
                    shifted = jnp.where(near, roll(cells, -b), roll(cells, -b - 4))
                    for a in range(7):
                        if 0 <= j - a < rows:
                            total[j - a] = total[j - a] + weights[a] * shifted
            for j in range(rows):
                conv[j, at, :] = total[j]
        for j in range(rows):
            at = (j // per, j % per) if split else (j,)
            sent[at + (both, slice(None))] = conv[j, both, :].astype(BF16)
        start = start_swap if split else start_gather
        start(ways, sent, every, send, recv, (slice(None), both))

    finish = finish_swap if split else finish_gather
    finish(ways, sent, every, send, recv)


def mix(lev, every, tall_ref, up_ref, upb_ref, down_ref, branch, back=None, send=None, recv=None):
    ways, count, chans, _ = every.shape
    own_count = ways * chans if back is not None else chans
    own = slice(None)
    if back is None:
        own = pl.ds(pl.multiple_of(lax.axis_index("chan") * chans, chans), chans)
    hidden_size = up_ref.shape[1]
    step = 256

    @pl.loop(0, count // 2)
    def _(i):
        sides = []
        for jj in range(2):
            values = every[:, 2 * i + jj].astype(F32).reshape(ways * chans, LANES)
            mean = jnp.sum(values, axis=0, keepdims=True) * (1.0 / (ways * chans))
            centred = values - mean
            spread = jnp.sum(centred * centred, axis=0, keepdims=True) * (1.0 / (ways * chans))
            scaled = centred * lax.rsqrt(spread + norm_eps)
            sides.append((scaled * tall_ref[:, lev : lev + 1] + tall_ref[:, 2 + lev : 3 + lev]).astype(BF16))
        normed = jnp.concatenate(sides, axis=1)
        total = jnp.broadcast_to(tall_ref[own, 4 + lev : 5 + lev], (own_count, 2 * LANES))
        for h in range(hidden_size // step):
            at = slice(h * step, (h + 1) * step)
            hidden = jnp.dot(up_ref[lev, at, :], normed, preferred_element_type=F32) + upb_ref[at, lev : lev + 1]
            hidden = 0.5 * hidden * (1.0 + lax.erf(hidden * (0.5**0.5)))
            total = total + jnp.dot(down_ref[lev, own, at], hidden.astype(BF16), preferred_element_type=F32)
        for jj in range(2):
            half = total[:, jj * LANES : (jj + 1) * LANES]
            if back is None:
                branch[2 * i + jj] = half
            else:
                branch[:, 2 * i + jj] = half.reshape(ways, chans, LANES).astype(BF16)
        if back is not None:
            start_swap(ways, branch, back, send, recv, (pl.ds(2 * i, 2),))

    if back is not None:
        finish_swap(ways, branch, back, send, recv)


def columns(block):
    return jnp.transpose(block)


def step_kernel(
    tiles,
    ways,
    wet_ref,
    device_of_ref,
    features_ref,
    land_ref,
    taps_ref,
    bias_ref,
    gain_ref,
    shift_ref,
    up_ref,
    up_bias_ref,
    down_ref,
    down_bias_ref,
    scale_ref,
    pool_ref,
    spread_ref,
    out_ref,
    table_v,
    table_s,
    rows_a,
    rows_b,
    rows_c,
    cols,
    tall,
    upb,
    mask,
    mask1,
    gather,
    grid0,
    grid1,
    rim0,
    rim1,
    units0,
    units1,
    outgoing0,
    outgoing1,
    held0,
    held1,
    picked0,
    picked1,
    got0,
    got1,
    conv,
    sent0,
    sent1,
    every0,
    every1,
    branch0,
    branch1,
    back0,
    fine,
    flat,
    sems,
    swaps,
):
    me = lax.axis_index("tile")
    chan = lax.axis_index("chan")
    pieces = outgoing0.shape[0]
    chans = grid0.shape[1]
    piece = (me * pieces + tiles - 1) // tiles
    holds = jnp.logical_and(piece < pieces, (piece * tiles) // pieces == me)
    barrier = pltpu.get_barrier_semaphore()

    @pl.when(holds)
    def _():
        def greet(targets):
            for target in targets:
                pl.semaphore_signal(barrier, inc=1, device_id={"tile": target}, device_id_type=MESH)

        each_other_tile(me, tiles, greet)

    @pl.when(jnp.logical_not(holds))
    def _():
        def greet(p):
            pl.semaphore_signal(barrier, inc=1, device_id={"tile": (p * tiles) // pieces}, device_id_type=MESH)

        each_piece(me, pieces, tiles, greet)

    for k in range(1, ways):
        pl.semaphore_signal(barrier, inc=1, device_id={"chan": lax.rem(chan + k, ways)}, device_id_type=MESH)

    lane = lane_ids()
    half = TILE * TILE // 2
    flat[...] = features_ref[...].astype(F32)
    for j in range(FINE.rows):
        grid0[3 + j] = jnp.zeros(grid0.shape[1:], F32)
        grid0[3 + j, :, 3 : 3 + TILE] = flat[:, TILE * j : TILE * (j + 1)]
        grid0[3 + j, :, 67 : 67 + TILE] = flat[:, half + TILE * j : half + TILE * (j + 1)]
    for outgoing in (outgoing0, outgoing1):
        outgoing[...] = jnp.zeros(outgoing.shape, BF16)
    cut_units(FINE, grid0, units0, outgoing0)

    @pl.when(holds)
    def _():
        pl.semaphore_wait(barrier, tiles - 1 + ways - 1)

    @pl.when(jnp.logical_not(holds))
    def _():
        pl.semaphore_wait(barrier, pieces + ways - 1)

    scatter_strips(FINE, tiles, outgoing0, held0, sems.at[0], sems.at[1])

    fold = source_table(2 * tiles // GRID_Y, GRID_Y, wet_ref, device_of_ref, table_v)
    table_copy = pltpu.make_async_copy(table_v, table_s, sems.at[8])
    table_copy.start()
    table_copy.wait()
    serve_strips(FINE, tiles, table_s, outgoing0, held0, picked0, got0, sems.at[1], sems.at[2], sems.at[3])
    rows_a[...] = jnp.zeros(rows_a.shape, F32)
    for at, ref in ((0, bias_ref), (2, scale_ref), (4, pool_ref), (8, spread_ref)):
        rows_a[at : at + ref.shape[0], :chans] = ref[...]
    cols[...] = columns(rows_a[...])[:chans]
    close_parts(FINE, grid0)
    depthwise_inside(FINE, 0, grid0, taps_ref, cols, conv)
    rows_b[...] = jnp.zeros(rows_b.shape, F32)
    for at, ref in ((0, gain_ref), (2, shift_ref), (4, down_bias_ref)):
        rows_b[at : at + 2, : ways * chans] = ref[...]
    tall[...] = columns(rows_b[...])[: ways * chans]
    rows_c[...] = jnp.zeros(rows_c.shape, F32)
    rows_c[0:2, :] = up_bias_ref[...]
    upb[...] = columns(rows_c[...])
    flat[0:1, :] = land_ref[...].astype(F32)
    for j in range(FINE.rows):
        mask[j] = jnp.zeros((1, LANES), F32)
        mask[j, :, :TILE] = flat[0:1, TILE * j : TILE * (j + 1)]
        mask[j, :, 64 : 64 + TILE] = flat[0:1, half + TILE * j : half + TILE * (j + 1)]
    source = lax.broadcasted_iota(jnp.int32, (2 * LANES, LANES), 0)
    target = lax.broadcasted_iota(jnp.int32, (2 * LANES, LANES), 1)
    block = lax.rem(source, LANES)
    wanted = 64 * (block // 64) + 32 * (source // LANES) + lax.rem(block, 64) // 2 + 3
    gather[...] = jnp.logical_and(
        target == wanted, jnp.logical_and(lax.rem(block, 2) == 0, lax.rem(block, 64) < TILE)
    ).astype(BF16)
    for j in range(COARSE.rows):
        sides = []
        for row in (j, j + COARSE.rows):
            value = jnp.broadcast_to(jnp.maximum(mask[2 * row], mask[2 * row + 1]), (8, LANES))
            sides.append(jnp.maximum(value, roll(value, -1)).astype(BF16))
        value = jnp.dot(jnp.concatenate(sides, axis=1), gather[...], preferred_element_type=F32)
        mask1[j] = roll(value, -3)[0:1]
    collect_strips(tiles, outgoing0, picked0, got0, sems.at[0], sems.at[2], sems.at[3])
    set_rim(FINE, rim0, units0, got0, fold)
    depthwise_rim(FINE, 0, ways, rim0, taps_ref, conv, sent0, every0, swaps.at[0], swaps.at[1])
    mix(0, every0, tall, up_ref, upb, down_ref, branch0, back0, swaps.at[2], swaps.at[3])
    per = sent0.shape[1]
    scale = cols[:, 2:3]
    for j in range(FINE.rows):
        value = roll(grid0[3 + j], -3) + scale * back0[j // per, j % per].astype(F32)
        fine[j] = (mask[j] * value).astype(BF16)
    pool = [cols[:, 4 + t : 5 + t] for t in range(4)]
    for j in range(COARSE.rows):
        sides = []
        for row in (j, j + COARSE.rows):
            low = fine[2 * row].astype(F32)
            high = fine[2 * row + 1].astype(F32)
            value = pool[0] * low + pool[1] * roll(low, -1) + pool[2] * high + pool[3] * roll(high, -1)
            sides.append(value.astype(BF16))
        grid1[3 + j] = jnp.dot(jnp.concatenate(sides, axis=1), gather[...], preferred_element_type=F32)
    cut_units(COARSE, grid1, units1, outgoing1)
    scatter_strips(COARSE, tiles, outgoing1, held1, sems.at[4], sems.at[5])
    serve_strips(COARSE, tiles, table_s, outgoing1, held1, picked1, got1, sems.at[5], sems.at[6], sems.at[7])
    close_parts(COARSE, grid1)
    depthwise_inside(COARSE, 1, grid1, taps_ref, cols, conv)
    collect_strips(tiles, outgoing1, picked1, got1, sems.at[4], sems.at[6], sems.at[7])
    set_rim(COARSE, rim1, units1, got1, fold)
    depthwise_rim(COARSE, 1, ways, rim1, taps_ref, conv, sent1, every1, swaps.at[4], swaps.at[5])
    mix(1, every1, tall, up_ref, upb, down_ref, branch1)
    scale = cols[:, 3:4]
    source = lax.broadcasted_iota(jnp.int32, (LANES, LANES), 0)
    target = lax.broadcasted_iota(jnp.int32, (LANES, LANES), 1)
    odd = lax.rem(lane, 2) == 1
    spread = [jnp.where(odd, cols[:, 9 + 2 * t : 10 + 2 * t], cols[:, 8 + 2 * t : 9 + 2 * t]) for t in range(2)]
    for j in range(COARSE.rows):
        value = roll(grid1[3 + j], -3) + scale * branch1[j]
        coarse = (mask1[j] * value).astype(BF16)
        for t in range(2):
            wanted = 64 * (target // 64) + 32 * t + lax.rem(target, 64) // 2
            scatter = jnp.logical_and(source == wanted, lax.rem(target, 64) < TILE).astype(BF16)
            wide = jnp.dot(coarse, scatter, preferred_element_type=F32)
            for row in range(2):
                at = 2 * (j + COARSE.rows * t) + row
                value = mask[at] * (fine[at].astype(F32) + spread[row] * wide)
                flat[:, TILE * at : TILE * (at + 1)] = value[:, :TILE]
                flat[:, half + TILE * at : half + TILE * (at + 1)] = value[:, 64 : 64 + TILE]
    out_ref[...] = flat[...].astype(BF16)


def per_device(
    ways,
    features,
    land_mask,
    wet_slots,
    device_of,
    depth_weight,
    depth_bias,
    norm_gain,
    norm_bias,
    up_weight,
    up_bias,
    down_weight,
    down_bias,
    layer_scale,
    pool_weight,
    spread_weight,
):
    tiles = wet_slots.shape[0]
    chans = features.shape[1]
    levels = (FINE, COARSE)
    scratch = [
        pltpu.VMEM((tiles, LANES), jnp.int32),
        pltpu.SMEM((tiles, LANES), jnp.int32),
        pltpu.VMEM((16, LANES), F32),
        pltpu.VMEM((8, 2 * LANES), F32),
        pltpu.VMEM((8, up_bias.shape[1]), F32),
        pltpu.VMEM((chans, 16), F32),
        pltpu.VMEM((ways * chans, 8), F32),
        pltpu.VMEM((up_bias.shape[1], 8), F32),
        pltpu.VMEM((FINE.rows, 1, LANES), F32),
        pltpu.VMEM((COARSE.rows, 1, LANES), F32),
        pltpu.VMEM((2 * LANES, LANES), BF16),
    ]
    scratch += [pltpu.VMEM((level.rows + 6, chans, LANES), F32) for level in levels] * 2
    scratch += [pltpu.VMEM((2, level.units, chans, LANES), BF16) for level in levels]
    scratch += [pltpu.VMEM((chans, level.units, 2, LANES), BF16) for level in levels]
    scratch += [pltpu.VMEM(((tiles + 1) * level.units, 2, LANES), BF16) for level in levels]
    scratch += [pltpu.VMEM((tiles, level.units, 2, LANES), BF16) for level in levels]
    scratch += [pltpu.VMEM((chans, level.units, 2, LANES), BF16) for level in levels]
    scratch += [pltpu.VMEM((FINE.rows, chans, LANES), F32)]
    quarter = pltpu.VMEM((ways, FINE.rows // ways, chans, LANES), BF16)
    scratch += [quarter, pltpu.VMEM((COARSE.rows, chans, LANES), BF16)]
    scratch += [quarter, pltpu.VMEM((ways, COARSE.rows, chans, LANES), BF16)]
    scratch += [quarter, pltpu.VMEM((COARSE.rows, chans, LANES), F32), quarter]
    scratch += [pltpu.VMEM((FINE.rows, chans, LANES), BF16), pltpu.VMEM((chans, TILE * TILE), F32)]
    scratch += [pltpu.SemaphoreType.DMA((9,)), pltpu.SemaphoreType.DMA((8, ways))]
    out = pl.pallas_call(
        functools.partial(step_kernel, tiles, ways),
        out_shape=jax.ShapeDtypeStruct(features.shape[1:], BF16),
        in_specs=[VMEM_SPEC] * 15,
        out_specs=VMEM_SPEC,
        scratch_shapes=scratch,
        compiler_params=pltpu.CompilerParams(
            collective_id=0, has_side_effects=True, vmem_limit_bytes=48 * 1024 * 1024
        ),
        name="ocean_step",
    )(
        wet_slots[None],
        device_of[None],
        features[0],
        land_mask,
        depth_weight,
        depth_bias,
        norm_gain,
        norm_bias,
        up_weight,
        up_bias,
        down_weight,
        down_bias,
        layer_scale,
        pool_weight.T,
        spread_weight.T,
    )
    return out[None]


def solution(mesh):
    placed = (
        P("tile", "chan", None),
        P("tile", None),
        P(),
        P(),
        P(None, "chan", None),
        P(None, "chan"),
        P(),
        P(),
        P(),
        P(),
        P(),
        P(),
        P(None, "chan"),
        P("chan", None),
        P("chan", None),
    )
    return jax.shard_map(
        functools.partial(per_device, mesh.shape["chan"]),
        mesh=mesh,
        in_specs=placed,
        out_specs=P("tile", "chan", None),
        check_vma=False,
    )
```

```python
import functools

import jax
import jax.numpy as jnp
from jax import lax
from jax.experimental import pallas as pl
from jax.experimental.pallas import tpu as pltpu
from jax.sharding import PartitionSpec as P

TILE = 48
GRID_Y = 4
MESH = pl.DeviceIdType.MESH
norm_eps = 1e-06
VMEM_SPEC = pl.BlockSpec(memory_space=pltpu.VMEM)
SMEM_SPEC = pl.BlockSpec(memory_space=pltpu.SMEM)
LANES = 128
F32 = jnp.float32
BF16 = jnp.bfloat16


class Level:
    def __init__(self, side, parts, slots):
        self.side = side
        self.parts = parts
        self.pitch = LANES // parts
        self.rows = side // parts
        self.slots = slots
        self.edge_units = -(-3 // parts)
        self.side_units = -(-self.rows // slots)
        self.units = max(2 * self.edge_units, self.side_units)


FINE = Level(TILE, 2, 8)
COARSE = Level(TILE // 2, 4, 3)


def roll(x, shift):
    shift %= LANES
    return x if shift == 0 else pltpu.roll(x, shift, x.ndim - 1)


def source_table(grid_x, grid_y, wet_ref, device_of_ref, table_ref):
    tiles = wet_ref.shape[1]
    wet = wet_ref[...]
    held_by = device_of_ref[...]
    device = lax.broadcasted_iota(jnp.int32, (tiles, tiles), 0)
    slot = jnp.sum(jnp.where(held_by == device, wet, 0), axis=1, keepdims=True)
    column = lax.rem(slot, grid_x)
    tile_row = lax.div(slot, grid_x)
    band = lax.broadcasted_iota(jnp.int32, (tiles, LANES), 1)
    up = jnp.where(band < 3, -1, jnp.where(band < 5, 0, 1))
    right = jnp.where(band < 3, band - 1, jnp.where(band < 5, 2 * band - 7, band - 6))
    near_row = tile_row + up
    folded = near_row >= grid_y
    right = jnp.where(folded, -right, right)
    near_column = lax.rem(column + right + grid_x, grid_x)
    source_column = jnp.where(folded, grid_x - 1 - near_column, near_column)
    source_row = jnp.where(folded, grid_y - 1, near_row)
    source_slot = jnp.where(near_row < 0, -1, source_row * grid_x + source_column)
    table = jnp.where(tile_row >= grid_y - 1, 1, jnp.zeros((tiles, LANES), jnp.int32))
    fold = jnp.where(device[:, :1] == lax.axis_index("tile"), table, 0)
    fold = jnp.sum(fold.astype(F32), axis=0, keepdims=True)
    for b in range(8):
        here = source_slot[:, b : b + 1] == wet
        found = jnp.sum(jnp.where(here, held_by + 1, 0), axis=1, keepdims=True)
        found = jnp.where(found > 0, found - 1, tiles)
        table = jnp.where(band == b, found, table)
    table_ref[...] = table
    return fold


def each_other_tile(me, tiles, body):
    layer = 16
    deep = tiles // layer
    mine = me // layer
    low = lax.rem(me, layer)

    @pl.loop(0, deep - 1)
    def _(n):
        half = (n + 1) // 2
        z = lax.rem(mine + deep // 2 + half * (2 * lax.rem(n, 2) - 1) + deep, deep)

        @pl.loop(0, layer // 4)
        def _(i):
            body([z * layer + lax.rem(low + layer // 2 + 4 * i + t, layer) for t in range(4)])

    @pl.loop(0, layer // 4 - 1)
    def _(i):
        body([mine * layer + lax.rem(low + 4 + 4 * i + t, layer) for t in range(4)])

    body([mine * layer + lax.rem(low + t, layer) for t in range(1, 4)])


def each_piece(me, pieces, tiles, body):
    start = (me * pieces) // tiles + pieces // 2

    @pl.loop(0, pieces // 2)
    def _(i):
        body(lax.rem(start + i, pieces))
        body(lax.rem(start + pieces - 1 - i, pieces))


def lane_ids(shape=(1, LANES)):
    return lax.broadcasted_iota(jnp.int32, shape, len(shape) - 1)


def cut_units(level, grid, units, outgoing):
    lane = lane_ids()
    q = lax.rem(lane, level.pitch)
    part = lane // level.pitch
    side, rows, pitch = level.side, level.rows, level.pitch

    def periodic(j):
        own = grid[j]
        own = jnp.where(q < 3, roll(own, -side), own)
        return jnp.where(q >= side + 3, roll(own, side), own)

    for edge in range(2):
        at = 0 if edge == 0 else level.parts - 1
        for unit in range(level.edge_units):
            value = None
            for k in range(3):
                if k // level.parts != unit:
                    continue
                row = roll(periodic((3 if edge == 0 else rows) + k), (k % level.parts - at) * pitch)
                value = row if value is None else jnp.where(part == k % level.parts, row, value)
            units[0, edge * level.edge_units + unit] = value.astype(BF16)
    for unit in range(level.side_units):
        value = None
        for slot in range(level.slots):
            j = unit * level.slots + slot
            if j >= rows:
                continue
            own = grid[3 + j]
            both = jnp.where(q < 6 * slot + 3, roll(own, 6 * slot - 3), roll(own, 6 * slot + 3 - side))
            value = both if value is None else jnp.where(q < 6 * slot, value, both)
        units[1, unit] = value.astype(BF16)
    for role in range(2):
        for unit in range((2 * level.edge_units, level.side_units)[role]):
            for p in range(outgoing.shape[0] // 2):
                outgoing[2 * p + role, unit] = units[role, unit, 2 * p : 2 * p + 2, :]
        for unit in range((2 * level.edge_units, level.side_units)[role], level.units):
            for p in range(outgoing.shape[0] // 2):
                outgoing[2 * p + role, unit] = jnp.zeros((2, LANES), BF16)


def scatter_strips(level, tiles, outgoing, held, send_a, recv_a):
    me = lax.axis_index("tile")
    pieces = outgoing.shape[0]
    units = level.units

    def send(p):
        target = (p * tiles) // pieces

        @pl.when(target != me)
        def _():
            pltpu.make_async_remote_copy(
                src_ref=outgoing.at[p],
                dst_ref=held.at[pl.ds(me * units, units)],
                send_sem=send_a,
                recv_sem=recv_a,
                device_id={"tile": target},
                device_id_type=MESH,
            ).start()

    each_piece(me, pieces, tiles, send)


def serve_strips(level, tiles, table_ref, outgoing, held, picked, got, recv_a, send_b, recv_b):
    me = lax.axis_index("tile")
    pieces = outgoing.shape[0]
    piece = (me * pieces + tiles - 1) // tiles
    holds = jnp.logical_and(piece < pieces, (piece * tiles) // pieces == me)
    units, edge = level.units, level.edge_units

    def send(target):
        pltpu.make_async_remote_copy(
            src_ref=picked.at[target],
            dst_ref=got.at[piece],
            send_sem=send_b,
            recv_sem=recv_b,
            device_id={"tile": target},
            device_id_type=MESH,
        ).start()

    @pl.when(holds)
    def _():
        held[pl.ds(tiles * units, units)] = jnp.zeros((units, 2, LANES), BF16)
        held[pl.ds(me * units, units)] = outgoing[piece]
        everything = held.at[pl.ds(0, (tiles - 1) * units)]
        pltpu.make_async_copy(everything, everything, recv_a).wait()
        q = lax.rem(lane_ids((2, LANES)), level.pitch)
        left_lanes = q < 3
        own_lanes = q < level.side + 3
        first_lanes = lax.rem(q, 6) < 3

        @pl.when(lax.rem(piece, 2) == 0)
        def _():
            def pick(target):
                below = [table_ref[target, band] * units + edge for band in range(3)]
                fold = table_ref[target, 8] * edge
                above = [table_ref[target, band] * units + fold for band in range(5, 8)]
                for unit in range(edge):
                    for base, place in ((below, unit), (above, edge + unit)):
                        left = held[base[0] + unit].astype(F32)
                        own = held[base[1] + unit].astype(F32)
                        right = held[base[2] + unit].astype(F32)
                        row = jnp.where(left_lanes, left, jnp.where(own_lanes, own, right))
                        picked[target, place] = row.astype(BF16)

            def pick_and_send(targets):
                for target in targets:
                    pick(target)
                for target in targets:
                    send(target)

            each_other_tile(me, tiles, pick_and_send)
            pick(me)

        @pl.when(lax.rem(piece, 2) == 1)
        def _():
            def pick(target):
                at_left = table_ref[target, 3] * units
                at_right = table_ref[target, 4] * units
                for unit in range(level.side_units):
                    left = held[at_left + unit].astype(F32)
                    right = held[at_right + unit].astype(F32)
                    picked[target, unit] = jnp.where(first_lanes, right, left).astype(BF16)

            def pick_and_send(targets):
                for target in targets:
                    pick(target)
                for target in targets:
                    send(target)

            each_other_tile(me, tiles, pick_and_send)
            pick(me)

        got[piece] = picked[me]

def collect_strips(tiles, outgoing, picked, got, send_a, send_b, recv_b):
    me = lax.axis_index("tile")
    pieces = outgoing.shape[0]
    piece = (me * pieces + tiles - 1) // tiles
    holds = jnp.logical_and(piece < pieces, (piece * tiles) // pieces == me)

    @pl.when(holds)
    def _():
        others = outgoing.at[pl.ds(0, pieces - 1)]
        pltpu.make_async_copy(others, others, send_a).wait()
        arrived = got.at[pl.ds(0, pieces - 1)]
        pltpu.make_async_copy(arrived, arrived, recv_b).wait()
        gone = picked.at[pl.ds(0, tiles - 1)]
        pltpu.make_async_copy(gone, gone, send_b).wait()

    @pl.when(jnp.logical_not(holds))
    def _():
        pltpu.make_async_copy(outgoing, outgoing, send_a).wait()
        pltpu.make_async_copy(got, got, recv_b).wait()


def close_parts(level, grid):
    lane = lane_ids()
    rows, pitch = level.rows, level.pitch
    for k in range(3):
        grid[k] = jnp.where(lane < pitch, 0.0, roll(grid[rows + k], pitch))
        grid[rows + 3 + k] = jnp.where(lane >= LANES - pitch, 0.0, roll(grid[3 + k], -pitch))


def set_rim(level, rim, units, got, fold):
    for role in range(2):
        for unit in range((2 * level.edge_units, level.side_units)[role]):
            for p in range(got.shape[0] // 2):
                units[role, unit, 2 * p : 2 * p + 2, :] = got[2 * p + role, unit]
    lane = lane_ids()
    q = lax.rem(lane, level.pitch)
    side, rows, pitch, edge = level.side, level.rows, level.pitch, level.edge_units
    for unit in range(level.side_units):
        value = units[1, unit].astype(F32)
        for slot in range(level.slots):
            j = unit * level.slots + slot
            if j >= rows:
                continue
            own = jnp.where(q < 3, roll(value, -6 * slot - 3), 0.0)
            rim[3 + j] = jnp.where(q < side + 3, own, roll(value, side + 3 - 6 * slot))
    backwards = (
        lax.broadcasted_iota(jnp.int32, (LANES, LANES), 0) + lax.broadcasted_iota(jnp.int32, (LANES, LANES), 1)
        == side + 5
    ).astype(BF16)
    above = []
    mirrored = []
    for k in range(3):
        below = roll(units[0, k // level.parts].astype(F32), -(k % level.parts) * pitch)
        rim[k] = jnp.where(lane < pitch, below, roll(rim[rows + k], pitch))
        row = roll(units[0, edge + k // level.parts].astype(F32), -(k % level.parts) * pitch)
        above.append(row)
        mirrored.append(jnp.dot(row.astype(BF16), backwards, preferred_element_type=F32))
    for k in range(3):
        top = jnp.where(fold > 0.5, mirrored[2 - k], above[k])
        top = roll(top, LANES - pitch)
        rim[rows + 3 + k] = jnp.where(lane >= LANES - pitch, top, roll(rim[3 + k], -pitch))


def peers(ways):
    return sorted(range(1, ways), key=lambda k: -min(k, ways - k))


def start_swap(ways, source, target, send, recv, window):
    me = lax.axis_index("chan")
    for k in peers(ways):
        peer = lax.rem(me + k, ways)
        pltpu.make_async_remote_copy(
            src_ref=source.at[(peer,) + window],
            dst_ref=target.at[(me,) + window],
            send_sem=send.at[k],
            recv_sem=recv.at[k],
            device_id={"chan": peer},
            device_id_type=MESH,
        ).start()


def finish_swap(ways, source, target, send, recv):
    me = lax.axis_index("chan")
    target[me] = source[me]
    for k in range(1, ways):
        block = source.at[k]
        pltpu.make_async_copy(block, block, send.at[k]).wait()
        pltpu.make_async_copy(block, block, recv.at[k]).wait()


def start_gather(ways, source, target, send, recv, window):
    me = lax.axis_index("chan")
    for k in peers(ways):
        pltpu.make_async_remote_copy(
            src_ref=source.at[window],
            dst_ref=target.at[(me,) + window],
            send_sem=send.at[k],
            recv_sem=recv.at[k],
            device_id={"chan": lax.rem(me + k, ways)},
            device_id_type=MESH,
        ).start()


def finish_gather(ways, source, target, send, recv):
    target[lax.axis_index("chan")] = source[...]
    for k in range(1, ways):
        pltpu.make_async_copy(source, source, send.at[k]).wait()
        pltpu.make_async_copy(source, source, recv.at[k]).wait()


def depthwise_inside(level, lev, grid, taps_ref, cols, conv):
    rows = level.rows

    @pl.loop(0, grid.shape[1] // 8)
    def _(g):
        at = pl.ds(pl.multiple_of(g * 8, 8), 8)
        taps = taps_ref[lev, at, :]
        total = [jnp.broadcast_to(cols[at, lev : lev + 1], (8, LANES))] * rows
        for b in range(7):
            weights = [jnp.broadcast_to(taps[:, 7 * a + b : 7 * a + b + 1], (8, LANES)) for a in range(7)]
            for j in range(rows + 6):
                shifted = roll(grid[j, at, :], -b)
                for a in range(7):
                    if 0 <= j - a < rows:
                        total[j - a] = total[j - a] + weights[a] * shifted
        for j in range(rows):
            conv[j, at, :] = total[j]


def depthwise_rim(level, lev, ways, rim, taps_ref, conv, sent, every, send, recv):
    rows = level.rows
    split = len(sent.shape) == 4
    per = sent.shape[1] if split else rows
    wide = 16
    near = lax.rem(lane_ids((8, LANES)), level.pitch) < 8

    @pl.loop(0, rim.shape[1] // wide)
    def _(g):
        both = pl.ds(pl.multiple_of(g * wide, wide), wide)
        for part in range(2):
            at = pl.ds(pl.multiple_of(g * wide + part * 8, 8), 8)
            taps = taps_ref[lev, at, :]
            total = [conv[j, at, :] for j in range(rows)]

            def tap(a, b):
                return jnp.broadcast_to(taps[:, 7 * a + b : 7 * a + b + 1], (8, LANES))

            for b in range(7):
                weights = [tap(a, b) for a in range(7)]
                for j in (0, 1, 2, rows + 3, rows + 4, rows + 5):
                    shifted = roll(rim[j, at, :], -b)
                    for a in range(7):
                        if 0 <= j - a < rows:
                            total[j - a] = total[j - a] + weights[a] * shifted
            for b in range(3):
                weights = [jnp.where(near, tap(a, b), tap(a, b + 4)) for a in range(7)]
                for j in range(3, rows + 3):
                    cells = rim[j, at, :]
                    shifted = jnp.where(near, roll(cells, -b), roll(cells, -b - 4))
                    for a in range(7):
                        if 0 <= j - a < rows:
                            total[j - a] = total[j - a] + weights[a] * shifted
            for j in range(rows):
                conv[j, at, :] = total[j]
        for j in range(rows):
            at = (j // per, j % per) if split else (j,)
            sent[at + (both, slice(None))] = conv[j, both, :].astype(BF16)
        start = start_swap if split else start_gather
        start(ways, sent, every, send, recv, (slice(None), both))

    finish = finish_swap if split else finish_gather
    finish(ways, sent, every, send, recv)


def mix(lev, every, tall_ref, up_ref, upb_ref, down_ref, branch, back=None, send=None, recv=None):
    ways, count, chans, _ = every.shape
    own_count = ways * chans if back is not None else chans
    own = slice(None)
    if back is None:
        own = pl.ds(pl.multiple_of(lax.axis_index("chan") * chans, chans), chans)
    hidden_size = up_ref.shape[1]
    step = 256

    @pl.loop(0, count // 2)
    def _(i):
        sides = []
        for jj in range(2):
            values = every[:, 2 * i + jj].astype(F32).reshape(ways * chans, LANES)
            mean = jnp.sum(values, axis=0, keepdims=True) * (1.0 / (ways * chans))
            centred = values - mean
            spread = jnp.sum(centred * centred, axis=0, keepdims=True) * (1.0 / (ways * chans))
            scaled = centred * lax.rsqrt(spread + norm_eps)
            sides.append((scaled * tall_ref[:, lev : lev + 1] + tall_ref[:, 2 + lev : 3 + lev]).astype(BF16))
        normed = jnp.concatenate(sides, axis=1)
        total = jnp.broadcast_to(tall_ref[own, 4 + lev : 5 + lev], (own_count, 2 * LANES))
        for h in range(hidden_size // step):
            at = slice(h * step, (h + 1) * step)
            hidden = jnp.dot(up_ref[lev, at, :], normed, preferred_element_type=F32) + upb_ref[at, lev : lev + 1]
            hidden = 0.5 * hidden * (1.0 + lax.erf(hidden * (0.5**0.5)))
            total = total + jnp.dot(down_ref[lev, own, at], hidden.astype(BF16), preferred_element_type=F32)
        for jj in range(2):
            half = total[:, jj * LANES : (jj + 1) * LANES]
            if back is None:
                branch[2 * i + jj] = half
            else:
                branch[:, 2 * i + jj] = half.reshape(ways, chans, LANES).astype(BF16)
        if back is not None:
            start_swap(ways, branch, back, send, recv, (pl.ds(2 * i, 2),))

    if back is not None:
        finish_swap(ways, branch, back, send, recv)


def columns(block):
    return jnp.transpose(block)


def step_kernel(
    tiles,
    ways,
    wet_ref,
    device_of_ref,
    features_ref,
    land_ref,
    taps_ref,
    bias_ref,
    gain_ref,
    shift_ref,
    up_ref,
    up_bias_ref,
    down_ref,
    down_bias_ref,
    scale_ref,
    pool_ref,
    spread_ref,
    out_ref,
    table_v,
    table_s,
    rows_a,
    rows_b,
    rows_c,
    cols,
    tall,
    upb,
    mask,
    mask1,
    gather,
    scatter,
    grid0,
    grid1,
    rim0,
    rim1,
    units0,
    units1,
    outgoing0,
    outgoing1,
    held0,
    held1,
    picked0,
    picked1,
    got0,
    got1,
    conv,
    sent0,
    sent1,
    every0,
    every1,
    branch0,
    branch1,
    back0,
    fine,
    flat,
    sems,
    swaps,
):
    me = lax.axis_index("tile")
    chan = lax.axis_index("chan")
    pieces = outgoing0.shape[0]
    chans = grid0.shape[1]
    piece = (me * pieces + tiles - 1) // tiles
    holds = jnp.logical_and(piece < pieces, (piece * tiles) // pieces == me)
    barrier = pltpu.get_barrier_semaphore()

    @pl.when(holds)
    def _():
        def greet(targets):
            for target in targets:
                pl.semaphore_signal(barrier, inc=1, device_id={"tile": target}, device_id_type=MESH)

        each_other_tile(me, tiles, greet)

    @pl.when(jnp.logical_not(holds))
    def _():
        def greet(p):
            pl.semaphore_signal(barrier, inc=1, device_id={"tile": (p * tiles) // pieces}, device_id_type=MESH)

        each_piece(me, pieces, tiles, greet)

    for k in range(1, ways):
        pl.semaphore_signal(barrier, inc=1, device_id={"chan": lax.rem(chan + k, ways)}, device_id_type=MESH)

    lane = lane_ids()
    half = TILE * TILE // 2
    flat[...] = features_ref[...].astype(F32)
    for j in range(FINE.rows):
        grid0[3 + j] = jnp.zeros(grid0.shape[1:], F32)
        grid0[3 + j, :, 3 : 3 + TILE] = flat[:, TILE * j : TILE * (j + 1)]
        grid0[3 + j, :, 67 : 67 + TILE] = flat[:, half + TILE * j : half + TILE * (j + 1)]
    cut_units(FINE, grid0, units0, outgoing0)

    @pl.when(holds)
    def _():
        pl.semaphore_wait(barrier, tiles - 1 + ways - 1)

    @pl.when(jnp.logical_not(holds))
    def _():
        pl.semaphore_wait(barrier, pieces + ways - 1)

    scatter_strips(FINE, tiles, outgoing0, held0, sems.at[0], sems.at[1])

    fold = source_table(2 * tiles // GRID_Y, GRID_Y, wet_ref, device_of_ref, table_v)
    table_copy = pltpu.make_async_copy(table_v, table_s, sems.at[8])
    table_copy.start()
    table_copy.wait()
    serve_strips(FINE, tiles, table_s, outgoing0, held0, picked0, got0, sems.at[1], sems.at[2], sems.at[3])
    rows_a[...] = jnp.zeros(rows_a.shape, F32)
    for at, ref in ((0, bias_ref), (2, scale_ref), (4, pool_ref), (8, spread_ref)):
        rows_a[at : at + ref.shape[0], :chans] = ref[...]
    cols[...] = columns(rows_a[...])[:chans]
    close_parts(FINE, grid0)
    depthwise_inside(FINE, 0, grid0, taps_ref, cols, conv)
    rows_b[...] = jnp.zeros(rows_b.shape, F32)
    for at, ref in ((0, gain_ref), (2, shift_ref), (4, down_bias_ref)):
        rows_b[at : at + 2, : ways * chans] = ref[...]
    tall[...] = columns(rows_b[...])[: ways * chans]
    rows_c[...] = jnp.zeros(rows_c.shape, F32)
    rows_c[0:2, :] = up_bias_ref[...]
    upb[...] = columns(rows_c[...])
    flat[0:1, :] = land_ref[...].astype(F32)
    for j in range(FINE.rows):
        mask[j] = jnp.zeros((1, LANES), F32)
        mask[j, :, :TILE] = flat[0:1, TILE * j : TILE * (j + 1)]
        mask[j, :, 64 : 64 + TILE] = flat[0:1, half + TILE * j : half + TILE * (j + 1)]
    source = lax.broadcasted_iota(jnp.int32, (2 * LANES, LANES), 0)
    target = lax.broadcasted_iota(jnp.int32, (2 * LANES, LANES), 1)
    block = lax.rem(source, LANES)
    wanted = 64 * (block // 64) + 32 * (source // LANES) + lax.rem(block, 64) // 2 + 3
    gather[...] = jnp.logical_and(
        target == wanted, jnp.logical_and(lax.rem(block, 2) == 0, lax.rem(block, 64) < TILE)
    ).astype(BF16)
    for j in range(COARSE.rows):
        sides = []
        for row in (j, j + COARSE.rows):
            value = jnp.broadcast_to(jnp.maximum(mask[2 * row], mask[2 * row + 1]), (8, LANES))
            sides.append(jnp.maximum(value, roll(value, -1)).astype(BF16))
        value = jnp.dot(jnp.concatenate(sides, axis=1), gather[...], preferred_element_type=F32)
        mask1[j] = roll(value, -3)[0:1]
    collect_strips(tiles, outgoing0, picked0, got0, sems.at[0], sems.at[2], sems.at[3])
    set_rim(FINE, rim0, units0, got0, fold)
    depthwise_rim(FINE, 0, ways, rim0, taps_ref, conv, sent0, every0, swaps.at[0], swaps.at[1])
    mix(0, every0, tall, up_ref, upb, down_ref, branch0, back0, swaps.at[2], swaps.at[3])
    per = sent0.shape[1]
    scale = cols[:, 2:3]
    for j in range(FINE.rows):
        value = roll(grid0[3 + j], -3) + scale * back0[j // per, j % per].astype(F32)
        fine[j] = (mask[j] * value).astype(BF16)
    pool = [cols[:, 4 + t : 5 + t] for t in range(4)]
    for j in range(COARSE.rows):
        sides = []
        for row in (j, j + COARSE.rows):
            low = fine[2 * row].astype(F32)
            high = fine[2 * row + 1].astype(F32)
            value = pool[0] * low + pool[1] * roll(low, -1) + pool[2] * high + pool[3] * roll(high, -1)
            sides.append(value.astype(BF16))
        grid1[3 + j] = jnp.dot(jnp.concatenate(sides, axis=1), gather[...], preferred_element_type=F32)
    cut_units(COARSE, grid1, units1, outgoing1)
    scatter_strips(COARSE, tiles, outgoing1, held1, sems.at[4], sems.at[5])
    serve_strips(COARSE, tiles, table_s, outgoing1, held1, picked1, got1, sems.at[5], sems.at[6], sems.at[7])
    close_parts(COARSE, grid1)
    depthwise_inside(COARSE, 1, grid1, taps_ref, cols, conv)
    source = lax.broadcasted_iota(jnp.int32, (LANES, LANES), 0)
    target = lax.broadcasted_iota(jnp.int32, (LANES, LANES), 1)
    for t in range(2):
        wanted = 64 * (target // 64) + 32 * t + lax.rem(target, 64) // 2
        scatter[t] = jnp.logical_and(source == wanted, lax.rem(target, 64) < TILE).astype(BF16)
    collect_strips(tiles, outgoing1, picked1, got1, sems.at[4], sems.at[6], sems.at[7])
    set_rim(COARSE, rim1, units1, got1, fold)
    depthwise_rim(COARSE, 1, ways, rim1, taps_ref, conv, sent1, every1, swaps.at[4], swaps.at[5])
    mix(1, every1, tall, up_ref, upb, down_ref, branch1)
    scale = cols[:, 3:4]
    odd = lax.rem(lane, 2) == 1
    spread = [jnp.where(odd, cols[:, 9 + 2 * t : 10 + 2 * t], cols[:, 8 + 2 * t : 9 + 2 * t]) for t in range(2)]
    for j in range(COARSE.rows):
        value = roll(grid1[3 + j], -3) + scale * branch1[j]
        coarse = (mask1[j] * value).astype(BF16)
        for t in range(2):
            wide = jnp.dot(coarse, scatter[t], preferred_element_type=F32)
            for row in range(2):
                at = 2 * (j + COARSE.rows * t) + row
                value = mask[at] * (fine[at].astype(F32) + spread[row] * wide)
                flat[:, TILE * at : TILE * (at + 1)] = value[:, :TILE]
                flat[:, half + TILE * at : half + TILE * (at + 1)] = value[:, 64 : 64 + TILE]
    out_ref[...] = flat[...].astype(BF16)


def per_device(
    ways,
    features,
    land_mask,
    wet_slots,
    device_of,
    depth_weight,
    depth_bias,
    norm_gain,
    norm_bias,
    up_weight,
    up_bias,
    down_weight,
    down_bias,
    layer_scale,
    pool_weight,
    spread_weight,
):
    tiles = wet_slots.shape[0]
    chans = features.shape[1]
    levels = (FINE, COARSE)
    scratch = [
        pltpu.VMEM((tiles, LANES), jnp.int32),
        pltpu.SMEM((tiles, LANES), jnp.int32),
        pltpu.VMEM((16, LANES), F32),
        pltpu.VMEM((8, 2 * LANES), F32),
        pltpu.VMEM((8, up_bias.shape[1]), F32),
        pltpu.VMEM((chans, 16), F32),
        pltpu.VMEM((ways * chans, 8), F32),
        pltpu.VMEM((up_bias.shape[1], 8), F32),
        pltpu.VMEM((FINE.rows, 1, LANES), F32),
        pltpu.VMEM((COARSE.rows, 1, LANES), F32),
        pltpu.VMEM((2 * LANES, LANES), BF16),
        pltpu.VMEM((2, LANES, LANES), BF16),
    ]
    scratch += [pltpu.VMEM((level.rows + 6, chans, LANES), F32) for level in levels] * 2
    scratch += [pltpu.VMEM((2, level.units, chans, LANES), BF16) for level in levels]
    scratch += [pltpu.VMEM((chans, level.units, 2, LANES), BF16) for level in levels]
    scratch += [pltpu.VMEM(((tiles + 1) * level.units, 2, LANES), BF16) for level in levels]
    scratch += [pltpu.VMEM((tiles, level.units, 2, LANES), BF16) for level in levels]
    scratch += [pltpu.VMEM((chans, level.units, 2, LANES), BF16) for level in levels]
    scratch += [pltpu.VMEM((FINE.rows, chans, LANES), F32)]
    quarter = pltpu.VMEM((ways, FINE.rows // ways, chans, LANES), BF16)
    scratch += [quarter, pltpu.VMEM((COARSE.rows, chans, LANES), BF16)]
    scratch += [quarter, pltpu.VMEM((ways, COARSE.rows, chans, LANES), BF16)]
    scratch += [quarter, pltpu.VMEM((COARSE.rows, chans, LANES), F32), quarter]
    scratch += [pltpu.VMEM((FINE.rows, chans, LANES), BF16), pltpu.VMEM((chans, TILE * TILE), F32)]
    scratch += [pltpu.SemaphoreType.DMA((9,)), pltpu.SemaphoreType.DMA((8, ways))]
    out = pl.pallas_call(
        functools.partial(step_kernel, tiles, ways),
        out_shape=jax.ShapeDtypeStruct(features.shape[1:], BF16),
        in_specs=[VMEM_SPEC] * 15,
        out_specs=VMEM_SPEC,
        scratch_shapes=scratch,
        compiler_params=pltpu.CompilerParams(
            collective_id=0, has_side_effects=True, vmem_limit_bytes=48 * 1024 * 1024
        ),
        name="ocean_step",
    )(
        wet_slots[None],
        device_of[None],
        features[0],
        land_mask,
        depth_weight,
        depth_bias,
        norm_gain,
        norm_bias,
        up_weight,
        up_bias,
        down_weight,
        down_bias,
        layer_scale,
        pool_weight.T,
        spread_weight.T,
    )
    return out[None]


def solution(mesh):
    placed = (
        P("tile", "chan", None),
        P("tile", None),
        P(),
        P(),
        P(None, "chan", None),
        P(None, "chan"),
        P(),
        P(),
        P(),
        P(),
        P(),
        P(),
        P(None, "chan"),
        P("chan", None),
        P("chan", None),
    )
    return jax.shard_map(
        functools.partial(per_device, mesh.shape["chan"]),
        mesh=mesh,
        in_specs=placed,
        out_specs=P("tile", "chan", None),
        check_vma=False,
    )
```
